256 devices in a mesh: depth: 16 (over x_hi, y, core), strip: 16 (over x_lo, z).
Axes of the slice: x: 4 (x_hi: 2, x_lo: 2; x = x_hi * 2 + x_lo), y: 4, z: 8, core: 2. Of those that a mesh axis runs over, the one named last changes fastest.
Arguments:
- volume: float32 [64, 1920, 1920], P('depth', 'strip'), may hold values from 0.001 to 4
- measured: float32 [1920, 1920], P('strip'), may hold values from 0.064 to 0.64
- row_taps: float32 [64, 31], P('depth'), may hold values from 0.009677419 to 0.09677419
- col_taps: float32 [64, 15, 31], P('depth'), may hold values from 0.009677419 to 0.09677419
- phase_map: int32 [64, 15], P('depth'), may hold values from 0 to 14
- radius: int32 [64], P('depth'), may hold values from 1 to 15, as said below
Outputs:
- volume_out: float32 [64, 1920, 1920], P('depth', 'strip')
The draws below stay inside these ranges and needn't reach their ends.
Inputs may be any that keep to these rules, and one draw needn't show every extreme that they name: Some plane's radius is exactly 15.
All inputs are finite; a program needn't handle non-finite values.
Results may differ from the reference program's by a relative error of at most 0.0032.
Values may be sent and summed in bfloat16 or wider, within the bound.
A program may use at most 128 MiB of HBM per device.

```python
import math
import jax
import jax.numpy as jnp
from jax import lax

P_SIZE = 15
NFAM = 15
RMAX = 15
ITERS = 2
TAPS = 31
NX = 1920
NY = 1920
NZ = 64


def shared_radius(key):
    spread_radii = jax.random.randint(jax.random.fold_in(key, 11), (NZ,), 1, RMAX + 1)
    widest = jax.random.randint(jax.random.fold_in(key, 12), (), 0, NZ)
    return jnp.where(jnp.arange(NZ) == widest, RMAX, spread_radii).astype(jnp.int32)


def draw_radius(key, part):
    return shared_radius(key)


def draw_volume(key, part):
    radii = shared_radius(key).astype(jnp.float32)
    footprint = (2.0 * radii + 1.0) * (2.0 * radii + 1.0)
    chance = 1.0 / footprint
    picker = jax.random.uniform(jax.random.fold_in(key, 21), (NZ, NY, NX), jnp.float32)
    levels = jax.random.uniform(jax.random.fold_in(key, 22), (NZ, NY, NX), jnp.float32)
    bright = jnp.exp(jnp.log(4.0) * levels)
    faint = 0.001 * jnp.exp(jnp.log(4.0) * levels)
    chosen = jnp.where(picker < chance[:, None, None], bright, faint)
    return jnp.clip(chosen, 0.001, 4.0).astype(jnp.float32)


def set_ends(entries, key, smallest, largest):
    spot = [jax.random.randint(jax.random.fold_in(key, axis), (), 0, length) for axis, length in enumerate(entries.shape)]
    longest = entries.shape.index(max(entries.shape))
    next_to = spot[:longest] + [(spot[longest] + 1) % entries.shape[longest]] + spot[longest + 1:]
    return entries.at[tuple(spot)].set(smallest).at[tuple(next_to)].set(largest)


def block_levels(rng, dims, split, low, high):
    level = 1.0
    for position, shards_of in split:
        steps = jax.random.uniform(jax.random.fold_in(jax.random.fold_in(rng, 6), position), (shards_of,), jnp.float32, low / len(split), high / len(split))
        level = level * jnp.repeat(jnp.exp(steps), dims[position] // shards_of).reshape((-1,) + (1,) * (len(dims) - 1 - position))
    return level


def setup_inputs(seed: int = 0) -> dict:
    key_list = jax.random.split(jax.random.key(seed), 7)
    return {
        "volume": draw_volume(jax.random.fold_in(key_list[6], 71), 0),
        "measured": jnp.clip(jnp.exp(math.log(0.64) - 2.30258502 * jax.random.uniform(key_list[1], (NY, NX), jnp.float32) ** block_levels(key_list[1], (NY, NX), ((0, 16),), -0.2, 0.2)), 0.064, 0.64),
        "row_taps": jnp.clip(jnp.exp(math.log(0.09677419) - 2.3025851 * jax.random.uniform(key_list[2], (NZ, TAPS), jnp.float32) ** block_levels(key_list[2], (NZ, TAPS), ((0, 16),), -0.2, 0.2)), 0.009677419, 0.09677419),
        "col_taps": jnp.clip(jnp.exp(math.log(0.09677419) - 2.3025851 * jax.random.uniform(key_list[3], (NZ, NFAM, TAPS), jnp.float32) ** block_levels(key_list[3], (NZ, NFAM, TAPS), ((0, 16),), -0.2, 0.2)), 0.009677419, 0.09677419),
        "phase_map": set_ends(jax.random.randint(key_list[4], (NZ, P_SIZE), 0, NFAM), jax.random.fold_in(key_list[4], 1), 0, NFAM - 1).astype(jnp.int32),
        "radius": draw_radius(jax.random.fold_in(key_list[6], 71), 0),
    }


def to_bf(value):
    return lax.optimization_barrier(value.astype(jnp.bfloat16)).astype(jnp.float32)


def displace(array, offset, axis_number):
    length = array.shape[axis_number]
    padding = [(0, 0)] * array.ndim
    padding[axis_number] = (max(offset, 0), max(-offset, 0))
    padded = jnp.pad(array, padding)
    return lax.slice_in_dim(padded, max(-offset, 0), max(-offset, 0) + length, axis=axis_number)


def plane_tables(row_tap, col_tap, phase_row, reach_limit):
    offsets = jnp.arange(TAPS, dtype=jnp.int32) - RMAX
    within = (jnp.abs(offsets) <= reach_limit).astype(jnp.float32)
    row_coef = to_bf(row_tap) * within
    family = phase_row[jnp.arange(NX, dtype=jnp.int32) % P_SIZE]
    col_coef = to_bf(col_tap[family]) * within[None, :]
    row_target = jnp.arange(NY, dtype=jnp.int32)[:, None] + offsets[None, :]
    row_grid = ((row_target >= 0) & (row_target < NY)).astype(jnp.float32)
    row_norm = jnp.sum(row_coef[None, :] * row_grid, axis=1)
    col_target = jnp.arange(NX, dtype=jnp.int32)[:, None] + offsets[None, :]
    col_grid = ((col_target >= 0) & (col_target < NX)).astype(jnp.float32)
    col_norm = jnp.sum(col_coef * col_grid, axis=1)
    return row_coef, col_coef, row_norm, col_norm


def reference(volume, measured, row_taps, col_taps, phase_map, radius):
    for iteration in range(ITERS):
        def project(sensor, plane):
            volume_plane, row_tap, col_tap, phase_row, reach_limit = plane
            row_coef, col_coef, row_norm, col_norm = plane_tables(row_tap, col_tap, phase_row, reach_limit)
            vol_bf = to_bf(volume_plane)
            spread = jnp.zeros((NY, NX), jnp.float32)
            for tap in range(TAPS):
                spread = spread + displace(vol_bf * col_coef[:, tap][None, :], tap - RMAX, 1)
            spread = to_bf(spread)
            for tap in range(TAPS):
                sensor = sensor + row_coef[tap] * displace(spread, tap - RMAX, 0)
            return sensor, None

        sensor, unused = lax.scan(project, jnp.zeros((NY, NX), jnp.float32),
                                  (volume, row_taps, col_taps, phase_map, radius))
        ratio_image = to_bf(measured / sensor)

        def update(plane):
            volume_plane, row_tap, col_tap, phase_row, reach_limit = plane
            row_coef, col_coef, row_norm, col_norm = plane_tables(row_tap, col_tap, phase_row, reach_limit)
            gathered = jnp.zeros((NY, NX), jnp.float32)
            for tap in range(TAPS):
                gathered = gathered + displace(ratio_image, RMAX - tap, 1) * col_coef[:, tap][None, :]
            gathered = to_bf(gathered)
            backproj = jnp.zeros((NY, NX), jnp.float32)
            for tap in range(TAPS):
                backproj = backproj + row_coef[tap] * displace(gathered, RMAX - tap, 0)
            return volume_plane * backproj / (row_norm[:, None] * col_norm[None, :])

        volume = lax.map(update, (volume, row_taps, col_taps, phase_map, radius))
    return volume
```

```python
import functools

import jax
import jax.numpy as jnp
from jax import lax
from jax.experimental import pallas as pl
from jax.experimental.pallas import tpu as pltpu
from jax.sharding import PartitionSpec as P

PITCH = 15
RMAX = 15
TAPS = 2 * RMAX + 1
ITERS = 2
LANE = 128
WIN = 256
BW = 225
HALO = 16
MESH = pl.DeviceIdType.MESH
BF = jnp.bfloat16
F32 = jnp.float32


def iota(shape, axis):
    return lax.broadcasted_iota(jnp.int32, shape, axis)


def dot(a, b):
    return jnp.dot(a, b, preferred_element_type=F32)


def unwindow(ref, k, rows):
    b0, l0 = divmod(LANE * k, BW)
    n0 = min(LANE, BW - l0)
    base = WIN * b0
    if l0 == 0:
        a = ref[:rows, base : base + LANE]
    elif l0 < LANE:
        a = pltpu.roll(ref[:rows, base : base + WIN], WIN - l0, axis=1)[:, :LANE]
    elif l0 == LANE:
        a = ref[:rows, base + LANE : base + WIN]
    else:
        a = pltpu.roll(ref[:rows, base + LANE : base + WIN], WIN - l0, axis=1)
    if n0 < LANE:
        b = pltpu.roll(ref[:rows, base + WIN : base + WIN + LANE], n0, axis=1)
        a = jnp.where(iota(a.shape, 1) < n0, a, b)
    return a


def kernel(depths, strips, vol_hbm, meas_hbm, rt_ref, ct_ref, pm_ref, rad_ref, out_hbm,
           v32, spr, pw, pc, sb, qb, rb, s_ref, hs, hb, mc, rc, wr, ga, bpw,
           ctf, up, fm, gm, bt, bfm, cinv, rinv,
           sem_vol, sem_out, sem_mc, sem_ms, sem_mr, sem_ps, sem_pr, sem_rs, sem_rr,
           sem_hs, sem_hr, sem_as, sem_ar, sem_fs, sem_fr):
    planes, rows, cols = vol_hbm.shape
    ext = rows + 2 * HALO
    kext = ga.shape[0]
    nb = -(-cols // BW)
    nk = cols // LANE
    chips = depths // 2
    d = lax.axis_index("depth")
    s = lax.axis_index("strip")
    c = lax.rem(d, 2)
    chip = d // 2
    sibling = d + 1 - 2 * c
    above = lax.rem(s + strips - 1, strips)
    below = lax.rem(s + 1, strips)
    peers = [lax.rem(chip + r, chips) for r in range(chips)]
    givers = [lax.rem(chip + chips - r, chips) for r in range(chips)]

    vol_in = []
    for z in range(planes):
        copy = pltpu.make_async_copy(
            vol_hbm.at[z], v32.at[z, 0:rows, LANE : LANE + cols], sem_vol.at[z]
        )
        copy.start()
        vol_in.append(copy)
    col0 = pl.multiple_of(jnp.minimum(d, nk - 1) * LANE, LANE)
    mc_in = pltpu.make_async_copy(
        meas_hbm.at[:, pl.ds(col0, LANE)], mc.at[HALO : HALO + rows, :], sem_mc
    )
    mc_in.start()

    barrier = pltpu.get_barrier_semaphore()
    pl.semaphore_signal(barrier, inc=1, device_id={"depth": sibling}, device_id_type=MESH)
    for r in range(1, chips):
        pl.semaphore_signal(
            barrier, inc=1, device_id={"depth": 2 * peers[r] + c}, device_id_type=MESH
        )
    for t in (above, below):
        pl.semaphore_signal(barrier, inc=1, device_id={"strip": t}, device_id_type=MESH)

    for z in range(planes):
        v32[z, rows:, :] = jnp.zeros((LANE - rows, v32.shape[2]), F32)
        v32[z, :, 0:LANE] = jnp.zeros((LANE, LANE), F32)
        v32[z, :, LANE + cols :] = jnp.zeros((LANE, v32.shape[2] - LANE - cols), F32)
    for it in range(ITERS):
        pc[it, nk] = jnp.zeros((ext, LANE), BF)
        rc[it, 0] = jnp.zeros((kext, LANE), BF)
        for k in range(1, nk + 2):
            rc[it, k, ext:, :] = jnp.zeros((kext - ext, LANE), BF)

    up[...] = jnp.zeros_like(up)
    every = jnp.where(lax.rem(iota((WIN, LANE), 0), PITCH) == iota((WIN, LANE), 1), 1.0, 0.0)
    every = every.astype(BF)
    inside = s * rows - HALO + iota((WIN, LANE), 0)
    inside = jnp.where((inside >= 0) & (inside < rows * strips), 1.0, 0.0).astype(BF)
    xs = BW * iota((16, WIN), 0) - RMAX + iota((16, WIN), 1)
    ones_win = jnp.where((xs >= 0) & (xs < cols), 1.0, 0.0).astype(BF)
    xo = BW * iota((16, WIN), 0) + iota((16, WIN), 1)
    col_ok = (xo < cols) & (iota((16, WIN), 1) < BW)
    row_ok = iota((LANE, LANE), 0) < rows
    for z in range(planes):
        reach = rad_ref[z]
        ctf[...] = jnp.zeros_like(ctf)
        keep = jnp.abs(iota((PITCH, TAPS), 1) - RMAX) <= reach
        ctf[0:PITCH, 0:TAPS] = jnp.where(keep, ct_ref[z], 0.0)
        keep1 = jnp.abs(iota((1, TAPS), 1) - RMAX) <= reach
        ctf[16:17, 0:TAPS] = jnp.where(keep1, rt_ref[z : z + 1, :], 0.0)
        family = jnp.full((16, LANE), -1, jnp.int32)
        for p in range(PITCH):
            family = jnp.where(iota((16, LANE), 0) == p, pm_ref[z, p], family)
        pick = jnp.where(family == iota((16, LANE), 1), 1.0, 0.0).astype(BF)
        table = ctf[...].astype(BF)
        up[0:16, :] = dot(pick, table)
        taps = dot(every, up[...].astype(BF))
        taps = jnp.concatenate([taps, jnp.zeros((WIN, WIN - LANE), F32)], axis=1)
        fwd = pltpu.roll(taps, 32 - 2 * RMAX, axis=1)
        fwd = pltpu.roll(fwd, WIN - 32, axis=1, stride=1, stride_axis=0)
        fm[z] = fwd.astype(BF)
        back = pltpu.roll(taps, 0, axis=1, stride=1, stride_axis=0)
        gm[z] = jnp.transpose(back).astype(BF)
        rtap = jnp.concatenate([ctf[16:17, :], jnp.zeros((1, WIN - LANE), F32)], axis=1)
        rtap = jnp.broadcast_to(rtap, (LANE, WIN))
        band = pltpu.roll(rtap, 1, axis=1)
        band = pltpu.roll(band, 0, axis=1, stride=1, stride_axis=0)
        bt[z] = band[:, :kext].astype(BF)
        bfm[:, LANE * z : LANE * (z + 1)] = jnp.transpose(band)[:kext, :].astype(BF)
        rn = dot(band.astype(BF), inside)
        rinv[z] = jnp.where(row_ok, 1.0 / rn, 0.0)
        cn = dot(ones_win, gm[z])
        cinv[z] = jnp.where(col_ok, 1.0 / cn, 0.0)

    pl.semaphore_wait(barrier, chips + 2)
    mc_in.wait()
    m_up = pltpu.make_async_remote_copy(
        src_ref=mc.at[HALO : 2 * HALO, :], dst_ref=mc.at[HALO + rows : ext, :],
        send_sem=sem_ms.at[0], recv_sem=sem_mr.at[0],
        device_id={"strip": above}, device_id_type=MESH,
    )
    m_down = pltpu.make_async_remote_copy(
        src_ref=mc.at[rows : rows + HALO, :], dst_ref=mc.at[0:HALO, :],
        send_sem=sem_ms.at[1], recv_sem=sem_mr.at[1],
        device_id={"strip": below}, device_id_type=MESH,
    )
    m_up.start()
    m_down.start()
    for copy in vol_in:
        copy.wait()

    def window(z, b):
        q, sh = divmod(LANE - RMAX + BW * b, LANE)
        x = v32[z, :, LANE * q : LANE * q + WIN + LANE]
        if sh:
            x = pltpu.roll(x, WIN + LANE - sh, axis=1)
        return x[:, :WIN].astype(BF)

    out_copies = []
    for it in range(ITERS):
        @pl.loop(0, planes)
        def _(z):
            for g in range(0, nb, 3):
                lhs = jnp.concatenate([window(z, b) for b in range(g, g + 3)], axis=0)
                res = dot(lhs, fm[z])
                for i in range(3):
                    spr[pl.ds(pl.multiple_of(z * LANE, LANE), LANE),
                        WIN * (g + i) : WIN * (g + i + 1)] = (
                        res[LANE * i : LANE * (i + 1)].astype(BF)
                    )

        pair = []
        done = 0
        for b in range(nb):
            pw[:, WIN * b : WIN * (b + 1)] = dot(bfm[...], spr[:, WIN * b : WIN * (b + 1)])
            while done < nk and (LANE * (done + 1) <= BW * (b + 1) or b == nb - 1):
                pc[it, done] = unwindow(pw, done, ext).astype(BF)
                done += 1
                if done % 2 == 0 or done == nk:
                    m = (done - 1) // 2
                    copy = pltpu.make_async_remote_copy(
                        src_ref=pc.at[it, 2 * m + 1 - c], dst_ref=sb.at[it, m],
                        send_sem=sem_ps.at[it, m], recv_sem=sem_pr.at[it, m],
                        device_id={"depth": sibling}, device_id_type=MESH,
                    )
                    copy.start()
                    pair.append(copy)

        for copy in pair:
            copy.wait_recv()
        spread_out = []
        for r in range(1, chips):
            k = peers[r]
            qb[it, r] = (pc[it, 2 * k + c].astype(F32) + sb[it, k].astype(F32)).astype(BF)
            copy = pltpu.make_async_remote_copy(
                src_ref=qb.at[it, r], dst_ref=rb.at[it, r],
                send_sem=sem_rs.at[it, r], recv_sem=sem_rr.at[it, r],
                device_id={"depth": 2 * k + c}, device_id_type=MESH,
            )
            copy.start()
            spread_out.append(copy)
        total = pc[it, d].astype(F32) + sb[it, chip].astype(F32)
        for copy in spread_out:
            copy.wait_recv()
        for r in range(1, chips):
            total = total + rb[it, r].astype(F32)
        s_ref[...] = total

        hs[it, 0] = s_ref[0 : 2 * HALO, :]
        hs[it, 1] = s_ref[rows:ext, :]
        h_up = pltpu.make_async_remote_copy(
            src_ref=hs.at[it, 0], dst_ref=hb.at[it, 1],
            send_sem=sem_hs.at[it, 0], recv_sem=sem_hr.at[it, 0],
            device_id={"strip": above}, device_id_type=MESH,
        )
        h_down = pltpu.make_async_remote_copy(
            src_ref=hs.at[it, 1], dst_ref=hb.at[it, 0],
            send_sem=sem_hs.at[it, 1], recv_sem=sem_hr.at[it, 1],
            device_id={"strip": below}, device_id_type=MESH,
        )
        h_up.start()
        h_down.start()
        if it == 0:
            m_up.wait()
            m_down.wait()
        h_up.wait()
        h_down.wait()
        s_ref[0 : 2 * HALO, :] = s_ref[0 : 2 * HALO, :] + jnp.where(s > 0, hb[it, 0], 0.0)
        s_ref[rows:ext, :] = s_ref[rows:ext, :] + jnp.where(s < strips - 1, hb[it, 1], 0.0)
        y = s * rows - HALO + iota((ext, LANE), 0)
        ok = (y >= 0) & (y < rows * strips) & (d < nk)
        rc[it, 1 + d, 0:ext, :] = jnp.where(ok, mc[...] / s_ref[...], 0.0).astype(BF)

        def give(slot, target, send, recv):
            return pltpu.make_async_remote_copy(
                src_ref=rc.at[it, slot, 0:ext, :], dst_ref=rc.at[it, slot, 0:ext, :],
                send_sem=send, recv_sem=recv,
                device_id={"depth": target}, device_id_type=MESH,
            )

        sent = []
        for r in range(1, chips):
            copy = give(1 + d, 2 * peers[r] + c, sem_as.at[it, r], sem_ar.at[it, r])
            copy.start()
            sent.append(copy)
        copy = give(1 + d, sibling, sem_fs.at[it, 0], sem_fr.at[it, 0])
        copy.start()
        sent.append(copy)
        for r in range(1, chips):
            slot = 1 + 2 * givers[r] + c
            give(slot, sibling, sem_as.at[it, r], sem_ar.at[it, r]).wait_recv()
            copy = give(slot, sibling, sem_fs.at[it, r], sem_fr.at[it, r])
            copy.start()
            sent.append(copy)
        for r in range(chips):
            slot = 1 + 2 * givers[r] + 1 - c
            give(slot, sibling, sem_fs.at[it, r], sem_fr.at[it, r]).wait_recv()

        for b in range(nb):
            q, sh = divmod(LANE - RMAX + BW * b, LANE)
            x = jnp.concatenate([rc[it, q + i].astype(F32) for i in range(3)], axis=1)
            if sh:
                x = pltpu.roll(x, WIN + LANE - sh, axis=1)
            wr[kext * b : kext * (b + 1), :] = x[:, :WIN].astype(BF)

        @pl.loop(0, planes)
        def _(z):
            for g in range(0, nb, 3):
                res = dot(wr[kext * g : kext * (g + 3), :], gm[z])
                for i in range(3):
                    ga[:, WIN * (g + i) : WIN * (g + i + 1)] = (
                        res[kext * i : kext * (i + 1)].astype(BF)
                    )
            scale = jnp.concatenate([rinv[z], rinv[z]], axis=1)
            for b in range(nb):
                bp = dot(bt[z], ga[:, WIN * b : WIN * (b + 1)])
                bpw[:, WIN * b : WIN * (b + 1)] = bp * scale * cinv[z, b : b + 1, :]
            for k in range(nk):
                at = slice(LANE * (k + 1), LANE * (k + 2))
                v32[z, :, at] = v32[z, :, at] * unwindow(bpw, k, LANE)
            if it == ITERS - 1:
                pltpu.make_async_copy(
                    v32.at[z, 0:rows, LANE : LANE + cols], out_hbm.at[z], sem_out.at[z]
                ).start()

        out_copies += pair + spread_out + sent

    for copy in out_copies:
        copy.wait_send()
    for z in range(planes):
        pltpu.make_async_copy(
            v32.at[z, 0:rows, LANE : LANE + cols], out_hbm.at[z], sem_out.at[z]
        ).wait()


def local(depths, strips, volume, measured, row_taps, col_taps, phase_map, radius):
    planes, rows, cols = volume.shape
    ext = rows + 2 * HALO
    kext = 160
    nb = -(-cols // BW)
    nk = cols // LANE
    chips = depths // 2
    dma = pltpu.SemaphoreType.DMA
    vmem = pltpu.VMEM
    return pl.pallas_call(
        functools.partial(kernel, depths, strips),
        out_shape=jax.ShapeDtypeStruct(volume.shape, F32),
        in_specs=[
            pl.BlockSpec(memory_space=pl.ANY),
            pl.BlockSpec(memory_space=pl.ANY),
            pl.BlockSpec(memory_space=pltpu.VMEM),
            pl.BlockSpec(memory_space=pltpu.VMEM),
            pl.BlockSpec(memory_space=pltpu.SMEM),
            pl.BlockSpec(memory_space=pltpu.SMEM),
        ],
        out_specs=pl.BlockSpec(memory_space=pl.ANY),
        scratch_shapes=[
            vmem((planes, LANE, cols + 2 * LANE), F32),
            vmem((planes * LANE, nb * WIN), BF),
            vmem((kext, nb * WIN), F32),
            vmem((ITERS, nk + 1, ext, LANE), BF),
            vmem((ITERS, chips, ext, LANE), BF),
            vmem((ITERS, chips, ext, LANE), BF),
            vmem((ITERS, chips, ext, LANE), BF),
            vmem((ext, LANE), F32),
            vmem((ITERS, 2, 2 * HALO, LANE), F32),
            vmem((ITERS, 2, 2 * HALO, LANE), F32),
            vmem((ext, LANE), F32),
            vmem((ITERS, nk + 2, kext, LANE), BF),
            vmem((nb * kext, WIN), BF),
            vmem((kext, nb * WIN), BF),
            vmem((LANE, nb * WIN), F32),
            vmem((LANE, LANE), F32),
            vmem((LANE, LANE), F32),
            vmem((planes, WIN, WIN), BF),
            vmem((planes, WIN, WIN), BF),
            vmem((planes, LANE, kext), BF),
            vmem((kext, planes * LANE), BF),
            vmem((planes, 16, WIN), F32),
            vmem((planes, LANE, LANE), F32),
            dma((planes,)),
            dma((planes,)),
            dma,
            dma((2,)),
            dma((2,)),
            dma((ITERS, chips)),
            dma((ITERS, chips)),
            dma((ITERS, chips)),
            dma((ITERS, chips)),
            dma((ITERS, 2)),
            dma((ITERS, 2)),
            dma((ITERS, chips)),
            dma((ITERS, chips)),
            dma((ITERS, chips)),
            dma((ITERS, chips)),
        ],
        compiler_params=pltpu.CompilerParams(
            collective_id=0, has_side_effects=True, vmem_limit_bytes=48 * 1024 * 1024
        ),
    )(volume, measured, row_taps, col_taps, phase_map, radius)


def solution(mesh):
    return jax.shard_map(
        functools.partial(local, mesh.shape["depth"], mesh.shape["strip"]),
        mesh=mesh,
        in_specs=(
            P("depth", "strip", None),
            P("strip", None),
            P("depth", None),
            P("depth", None, None),
            P("depth", None),
            P("depth"),
        ),
        out_specs=P("depth", "strip", None),
        check_vma=False,
    )
```

```python
import functools

import jax
import jax.numpy as jnp
from jax import lax
from jax.experimental import pallas as pl
from jax.experimental.pallas import tpu as pltpu
from jax.sharding import PartitionSpec as P

PITCH = 15
RMAX = 15
TAPS = 2 * RMAX + 1
ITERS = 2
LANE = 128
WIN = 256
BW = 225
HALO = 16
MESH = pl.DeviceIdType.MESH
BF = jnp.bfloat16
F32 = jnp.float32


def iota(shape, axis):
    return lax.broadcasted_iota(jnp.int32, shape, axis)


def dot(a, b):
    return jnp.dot(a, b, preferred_element_type=F32)


def unwindow(ref, k, rows):
    b0, l0 = divmod(LANE * k, BW)
    n0 = min(LANE, BW - l0)
    base = WIN * b0
    if l0 == 0:
        a = ref[:rows, base : base + LANE]
    elif l0 < LANE:
        a = pltpu.roll(ref[:rows, base : base + WIN], WIN - l0, axis=1)[:, :LANE]
    elif l0 == LANE:
        a = ref[:rows, base + LANE : base + WIN]
    else:
        a = pltpu.roll(ref[:rows, base + LANE : base + WIN], WIN - l0, axis=1)
    if n0 < LANE:
        b = pltpu.roll(ref[:rows, base + WIN : base + WIN + LANE], n0, axis=1)
        a = jnp.where(iota(a.shape, 1) < n0, a, b)
    return a


def kernel(depths, strips, vol_hbm, meas_hbm, rt_hbm, ct_hbm, pm_hbm, rad_hbm, out_hbm,
           rt_ref, ct_ref, pm_ref, rad_ref,
           v32, spr, pw, pc, sb, qb, rb, s_ref, hb, mc, rc, wr, ga, bpw,
           ctf, up, fm, gm, bt, bfm, cinv, rinv,
           sem_vol, sem_out, sem_in, sem_ms, sem_mr, sem_ps, sem_pr, sem_rs, sem_rr,
           sem_hs, sem_hr, sem_as, sem_ar, sem_fs, sem_fr):
    planes, rows, cols = vol_hbm.shape
    ext = rows + 2 * HALO
    kext = ga.shape[1]
    edge = 4 * HALO
    nb = -(-cols // BW)
    nk = cols // LANE
    chips = depths // 2
    d = lax.axis_index("depth")
    s = lax.axis_index("strip")
    c = lax.rem(d, 2)
    chip = d // 2
    sibling = d + 1 - 2 * c
    above = lax.rem(s + strips - 1, strips)
    below = lax.rem(s + 1, strips)
    peers = [lax.rem(chip + r, chips) for r in range(chips)]
    givers = [lax.rem(chip + chips - r, chips) for r in range(chips)]

    def strip_row(p):
        return jnp.where(p < 2 * HALO, p + rows - HALO, p - 3 * HALO)

    arg_in = []
    for i, (src, dst) in enumerate(
        ((rt_hbm, rt_ref), (ct_hbm, ct_ref), (pm_hbm, pm_ref), (rad_hbm, rad_ref))
    ):
        copy = pltpu.make_async_copy(src, dst, sem_in.at[i])
        copy.start()
        arg_in.append(copy)
    vol_in = []
    for z in range(planes):
        copy = pltpu.make_async_copy(
            vol_hbm.at[z], v32.at[z, 0:rows, LANE : LANE + cols], sem_vol.at[z]
        )
        copy.start()
        vol_in.append(copy)
    col0 = pl.multiple_of(jnp.minimum(d, nk - 1) * LANE, LANE)
    mc_in = [
        pltpu.make_async_copy(
            meas_hbm.at[0 : rows - HALO, pl.ds(col0, LANE)], mc.at[3 * HALO : ext, :], sem_in.at[4]
        ),
        pltpu.make_async_copy(
            meas_hbm.at[rows - HALO : rows, pl.ds(col0, LANE)], mc.at[0:HALO, :], sem_in.at[5]
        ),
    ]
    for copy in mc_in:
        copy.start()

    barrier = pltpu.get_barrier_semaphore()
    pl.semaphore_signal(barrier, inc=1, device_id={"depth": sibling}, device_id_type=MESH)
    for r in range(1, chips):
        pl.semaphore_signal(
            barrier, inc=1, device_id={"depth": 2 * peers[r] + c}, device_id_type=MESH
        )
    for t in (above, below):
        pl.semaphore_signal(barrier, inc=1, device_id={"strip": t}, device_id_type=MESH)

    for z in range(planes):
        v32[z, rows:, :] = jnp.zeros((LANE - rows, v32.shape[2]), F32)
        v32[z, :, 0:LANE] = jnp.zeros((LANE, LANE), F32)
        v32[z, :, LANE + cols :] = jnp.zeros((LANE, v32.shape[2] - LANE - cols), F32)
    for it in range(ITERS):
        pc[it, nk] = jnp.zeros((ext, LANE), BF)
        rc[it, 0] = jnp.zeros((kext, LANE), BF)
        for k in range(1, nk + 2):
            rc[it, k, ext:, :] = jnp.zeros((kext - ext, LANE), BF)

    up[...] = jnp.zeros_like(up)
    every = jnp.where(lax.rem(iota((WIN, LANE), 0), PITCH) == iota((WIN, LANE), 1), 1.0, 0.0)
    every = every.astype(BF)
    y = s * rows + strip_row(iota((kext, LANE), 0))
    inside = (y >= 0) & (y < rows * strips) & (iota((kext, LANE), 0) < ext)
    inside = jnp.where(inside, 1.0, 0.0).astype(BF)
    xs = BW * iota((16, WIN), 0) - RMAX + iota((16, WIN), 1)
    ones_win = jnp.where((xs >= 0) & (xs < cols), 1.0, 0.0).astype(BF)
    xo = BW * iota((16, WIN), 0) + iota((16, WIN), 1)
    col_ok = (xo < cols) & (iota((16, WIN), 1) < BW)
    row_ok = iota((LANE, LANE), 0) < rows
    for copy in arg_in:
        copy.wait()
    for z in range(planes):
        reach = rad_ref[z]
        ctf[...] = jnp.zeros_like(ctf)
        keep = jnp.abs(iota((PITCH, TAPS), 1) - RMAX) <= reach
        ctf[0:PITCH, 0:TAPS] = jnp.where(keep, ct_ref[:, z, :], 0.0)
        keep1 = jnp.abs(iota((1, TAPS), 1) - RMAX) <= reach
        ctf[16:17, 0:TAPS] = jnp.where(keep1, rt_ref[z : z + 1, :], 0.0)
        family = jnp.full((16, LANE), -1, jnp.int32)
        for p in range(PITCH):
            family = jnp.where(iota((16, LANE), 0) == p, pm_ref[z, p], family)
        pick = jnp.where(family == iota((16, LANE), 1), 1.0, 0.0).astype(BF)
        table = ctf[...].astype(BF)
        up[0:16, :] = dot(pick, table)
        taps = dot(every, up[...].astype(BF))
        taps = jnp.concatenate([taps, jnp.zeros((WIN, WIN - LANE), F32)], axis=1)
        fwd = pltpu.roll(taps, 32 - 2 * RMAX, axis=1)
        fwd = pltpu.roll(fwd, WIN - 32, axis=1, stride=1, stride_axis=0)
        fm[z] = fwd.astype(BF)
        back = pltpu.roll(taps, 0, axis=1, stride=1, stride_axis=0)
        gm[z] = jnp.transpose(back).astype(BF)
        rtap = jnp.concatenate([ctf[16:17, :], jnp.zeros((1, WIN - LANE), F32)], axis=1)
        rtap = jnp.broadcast_to(rtap, (LANE, WIN))
        band = pltpu.roll(rtap, 1, axis=1)
        band = pltpu.roll(band, 0, axis=1, stride=1, stride_axis=0)
        p = iota((LANE, WIN), 1)
        last = pltpu.roll(band, WIN - rows, axis=1)
        band = jnp.where(p < 2 * HALO, last, pltpu.roll(band, 2 * HALO, axis=1))
        band = jnp.where(p < ext, band, 0.0)
        bt[z] = band[:, :kext].astype(BF)
        bfm[:, LANE * z : LANE * (z + 1)] = jnp.transpose(band)[:kext, :].astype(BF)
        rn = dot(bt[z], inside)
        rinv[z] = jnp.where(row_ok, 1.0 / rn, 0.0)
        cn = dot(ones_win, gm[z])
        cinv[z] = jnp.where(col_ok, 1.0 / cn, 0.0)

    pl.semaphore_wait(barrier, chips + 2)
    for copy in mc_in:
        copy.wait()
    m_up = pltpu.make_async_remote_copy(
        src_ref=mc.at[3 * HALO : 4 * HALO, :], dst_ref=mc.at[HALO : 2 * HALO, :],
        send_sem=sem_ms.at[0], recv_sem=sem_mr.at[0],
        device_id={"strip": above}, device_id_type=MESH,
    )
    m_down = pltpu.make_async_remote_copy(
        src_ref=mc.at[0:HALO, :], dst_ref=mc.at[2 * HALO : 3 * HALO, :],
        send_sem=sem_ms.at[1], recv_sem=sem_mr.at[1],
        device_id={"strip": below}, device_id_type=MESH,
    )
    m_up.start()
    m_down.start()
    for copy in vol_in:
        copy.wait()

    def window(z, b):
        q, sh = divmod(LANE - RMAX + BW * b, LANE)
        x = v32[z, :, LANE * q : LANE * q + WIN + LANE]
        if sh:
            x = pltpu.roll(x, WIN + LANE - sh, axis=1)
        return x[:, :WIN].astype(BF)

    out_copies = []
    for it in range(ITERS):
        @pl.loop(0, planes)
        def _(z):
            for g in range(0, nb, 3):
                lhs = jnp.concatenate([window(z, b) for b in range(g, g + 3)], axis=0)
                res = dot(lhs, fm[z])
                for i in range(3):
                    spr[pl.ds(pl.multiple_of(z * LANE, LANE), LANE),
                        WIN * (g + i) : WIN * (g + i + 1)] = (
                        res[LANE * i : LANE * (i + 1)].astype(BF)
                    )

        pair = []
        done = 0
        for b in range(nb):
            pw[:, WIN * b : WIN * (b + 1)] = dot(bfm[...], spr[:, WIN * b : WIN * (b + 1)])
            while done < nk and (LANE * (done + 1) <= BW * (b + 1) or b == nb - 1):
                pc[it, done] = unwindow(pw, done, ext).astype(BF)
                done += 1
                if done % 2 == 0 or done == nk:
                    m = (done - 1) // 2
                    copy = pltpu.make_async_remote_copy(
                        src_ref=pc.at[it, 2 * m + 1 - c], dst_ref=sb.at[it, m],
                        send_sem=sem_ps.at[it, m], recv_sem=sem_pr.at[it, m],
                        device_id={"depth": sibling}, device_id_type=MESH,
                    )
                    copy.start()
                    pair.append(copy)

        def paired(m):
            pltpu.make_async_remote_copy(
                src_ref=pc.at[it, 2 * m + 1 - c], dst_ref=sb.at[it, m],
                send_sem=sem_ps.at[it, m], recv_sem=sem_pr.at[it, m],
                device_id={"depth": sibling}, device_id_type=MESH,
            ).wait_recv()
            return pc[it, 2 * m + c].astype(F32) + sb[it, m].astype(F32)

        spread_out = []
        for r in range(1, chips):
            k = peers[r]
            qb[it, r] = paired(k).astype(BF)
            copy = pltpu.make_async_remote_copy(
                src_ref=qb.at[it, r], dst_ref=rb.at[it, r],
                send_sem=sem_rs.at[it, r], recv_sem=sem_rr.at[it, r],
                device_id={"depth": 2 * k + c}, device_id_type=MESH,
            )
            copy.start()
            spread_out.append(copy)
        total = paired(chip)
        for r in range(1, chips):
            spread_out[r - 1].wait_recv()
            total = total + rb[it, r].astype(F32)
        s_ref[it] = total

        h_up = pltpu.make_async_remote_copy(
            src_ref=s_ref.at[it, 2 * HALO : edge], dst_ref=hb.at[it, 0 : 2 * HALO],
            send_sem=sem_hs.at[it, 0], recv_sem=sem_hr.at[it, 0],
            device_id={"strip": above}, device_id_type=MESH,
        )
        h_down = pltpu.make_async_remote_copy(
            src_ref=s_ref.at[it, 0 : 2 * HALO], dst_ref=hb.at[it, 2 * HALO : edge],
            send_sem=sem_hs.at[it, 1], recv_sem=sem_hr.at[it, 1],
            device_id={"strip": below}, device_id_type=MESH,
        )
        h_up.start()
        h_down.start()

        def give(part, slot, target, send, recv):
            at = rc.at[it, slot, edge:ext, :] if part == 0 else rc.at[it, slot, 0:edge, :]
            return pltpu.make_async_remote_copy(
                src_ref=at, dst_ref=at, send_sem=send, recv_sem=recv,
                device_id={"depth": target}, device_id_type=MESH,
            )

        sent = []

        def give_own(part):
            for r in range(1, chips):
                copy = give(part, 1 + d, 2 * peers[r] + c,
                            sem_as.at[it, part, r], sem_ar.at[it, part, r])
                copy.start()
                sent.append(copy)
            copy = give(part, 1 + d, sibling, sem_fs.at[it, part, 0], sem_fr.at[it, part, 0])
            copy.start()
            sent.append(copy)

        def forward(part):
            for r in range(1, chips):
                slot = 1 + 2 * givers[r] + c
                give(part, slot, sibling,
                     sem_as.at[it, part, r], sem_ar.at[it, part, r]).wait_recv()
                copy = give(part, slot, sibling, sem_fs.at[it, part, r], sem_fr.at[it, part, r])
                copy.start()
                sent.append(copy)

        def arrived(part):
            for r in range(chips):
                slot = 1 + 2 * givers[r] + 1 - c
                give(part, slot, sibling,
                     sem_fs.at[it, part, r], sem_fr.at[it, part, r]).wait_recv()

        def back_windows(top, end):
            for b in range(nb):
                q, sh = divmod(LANE - RMAX + BW * b, LANE)
                x = jnp.concatenate(
                    [rc[it, q + i, top:end, :].astype(F32) for i in range(3)], axis=1
                )
                if sh:
                    x = pltpu.roll(x, WIN + LANE - sh, axis=1)
                wr[nb * top + (end - top) * b : nb * top + (end - top) * (b + 1), :] = (
                    x[:, :WIN].astype(BF)
                )

        def back_columns(z, top, end):
            n = end - top
            for g in range(0, nb, 3):
                res = dot(wr[nb * top + n * g : nb * top + n * (g + 3), :], gm[z])
                for i in range(3):
                    ga[z, top:end, WIN * (g + i) : WIN * (g + i + 1)] = (
                        res[n * i : n * (i + 1)].astype(BF)
                    )

        if it == 0:
            m_up.wait_recv()
            m_down.wait_recv()
        y = s * rows + strip_row(iota((ext, LANE), 0))
        ok = (y >= 0) & (y < rows * strips) & (d < nk)
        ratio = jnp.where(ok[edge:], mc[edge:, :] / s_ref[it, edge:, :], 0.0)
        rc[it, 1 + d, edge:ext, :] = ratio.astype(BF)
        give_own(0)
        h_up.wait_recv()
        h_down.wait_recv()
        first = iota((edge, LANE), 0) < 2 * HALO
        other = (first & (s < strips - 1)) | (~first & (s > 0))
        shared = s_ref[it, 0:edge, :] + jnp.where(other, hb[it], 0.0)
        ratio = jnp.where(ok[:edge], mc[0:edge, :] / shared, 0.0)
        rc[it, 1 + d, 0:edge, :] = ratio.astype(BF)
        give_own(1)
        forward(0)
        arrived(0)
        back_windows(edge, kext)
        forward(1)

        @pl.loop(0, planes)
        def _(z):
            back_columns(z, edge, kext)

        arrived(1)
        back_windows(0, edge)

        @pl.loop(0, planes)
        def _(z):
            back_columns(z, 0, edge)
            scale = jnp.concatenate([rinv[z], rinv[z]], axis=1)
            for b in range(nb):
                bp = dot(bt[z], ga[z, :, WIN * b : WIN * (b + 1)])
                bpw[:, WIN * b : WIN * (b + 1)] = bp * scale * cinv[z, b : b + 1, :]
            for k in range(nk):
                at = slice(LANE * (k + 1), LANE * (k + 2))
                v32[z, :, at] = v32[z, :, at] * unwindow(bpw, k, LANE)
            if it == ITERS - 1:
                pltpu.make_async_copy(
                    v32.at[z, 0:rows, LANE : LANE + cols], out_hbm.at[z], sem_out.at[z]
                ).start()

        out_copies += pair + spread_out + sent + [h_up, h_down]

    for copy in out_copies + [m_up, m_down]:
        copy.wait_send()
    for z in range(planes):
        pltpu.make_async_copy(
            v32.at[z, 0:rows, LANE : LANE + cols], out_hbm.at[z], sem_out.at[z]
        ).wait()


def local(depths, strips, volume, measured, row_taps, col_taps, phase_map, radius):
    planes, rows, cols = volume.shape
    ext = rows + 2 * HALO
    kext = 160
    nb = -(-cols // BW)
    nk = cols // LANE
    chips = depths // 2
    dma = pltpu.SemaphoreType.DMA
    vmem = pltpu.VMEM
    return pl.pallas_call(
        functools.partial(kernel, depths, strips),
        out_shape=jax.ShapeDtypeStruct(volume.shape, F32),
        in_specs=[pl.BlockSpec(memory_space=pltpu.HBM)] * 6,
        out_specs=pl.BlockSpec(memory_space=pl.ANY),
        scratch_shapes=[
            vmem(row_taps.shape, F32),
            vmem((PITCH, planes, TAPS), F32),
            pltpu.SMEM(phase_map.shape, jnp.int32),
            pltpu.SMEM(radius.shape, jnp.int32),
            vmem((planes, LANE, cols + 2 * LANE), F32),
            vmem((planes * LANE, nb * WIN), BF),
            vmem((kext, nb * WIN), F32),
            vmem((ITERS, nk + 1, ext, LANE), BF),
            vmem((ITERS, chips, ext, LANE), BF),
            vmem((ITERS, chips, ext, LANE), BF),
            vmem((ITERS, chips, ext, LANE), BF),
            vmem((ITERS, ext, LANE), F32),
            vmem((ITERS, 4 * HALO, LANE), F32),
            vmem((ext, LANE), F32),
            vmem((ITERS, nk + 2, kext, LANE), BF),
            vmem((nb * kext, WIN), BF),
            vmem((planes, kext, nb * WIN), BF),
            vmem((LANE, nb * WIN), F32),
            vmem((LANE, LANE), F32),
            vmem((LANE, LANE), F32),
            vmem((planes, WIN, WIN), BF),
            vmem((planes, WIN, WIN), BF),
            vmem((planes, LANE, kext), BF),
            vmem((kext, planes * LANE), BF),
            vmem((planes, 16, WIN), F32),
            vmem((planes, LANE, LANE), F32),
            dma((planes,)),
            dma((planes,)),
            dma((6,)),
            dma((2,)),
            dma((2,)),
            dma((ITERS, chips)),
            dma((ITERS, chips)),
            dma((ITERS, chips)),
            dma((ITERS, chips)),
            dma((ITERS, 2)),
            dma((ITERS, 2)),
            dma((ITERS, 2, chips)),
            dma((ITERS, 2, chips)),
            dma((ITERS, 2, chips)),
            dma((ITERS, 2, chips)),
        ],
        compiler_params=pltpu.CompilerParams(
            collective_id=0, has_side_effects=True, vmem_limit_bytes=48 * 1024 * 1024
        ),
    )(*(
        pltpu.with_memory_space_constraint(x, pltpu.HBM)
        for x in (volume, measured, row_taps, jnp.transpose(col_taps, (1, 0, 2)), phase_map, radius)
    ))


def solution(mesh):
    return jax.shard_map(
        functools.partial(local, mesh.shape["depth"], mesh.shape["strip"]),
        mesh=mesh,
        in_specs=(
            P("depth", "strip", None),
            P("strip", None),
            P("depth", None),
            P("depth", None, None),
            P("depth", None),
            P("depth"),
        ),
        out_specs=P("depth", "strip", None),
        check_vma=False,
    )
```

```python
import functools

import jax
import jax.numpy as jnp
from jax import lax
from jax.experimental import pallas as pl
from jax.experimental.pallas import tpu as pltpu
from jax.sharding import PartitionSpec as P

PITCH = 15
RMAX = 15
TAPS = 2 * RMAX + 1
ITERS = 2
LANE = 128
WIN = 256
BW = 225
FIRST = (0, 795)
SPREAD = (((0, 5), (1, 4)), ((0, 4), (0, 5)))
CHUNKS = (((0, 8), (8, 7)), ((0, 7), (7, 8)))
BACK = ((5, 5), (4, 5))
SPLIT = (1005, 870)
MOST = 5
HALO = 16
MESH = pl.DeviceIdType.MESH
BF = jnp.bfloat16
F32 = jnp.float32


def iota(shape, axis):
    return lax.broadcasted_iota(jnp.int32, shape, axis)


def dot(a, b):
    return jnp.dot(a, b, preferred_element_type=F32)


def unwindow(ref, k, rows, start):
    b0, l0 = divmod(LANE * k - start, BW)
    if b0 < 0:
        return pltpu.roll(ref[:rows, 0:LANE], start - LANE * k, axis=1)
    n0 = min(LANE, BW - l0)
    base = WIN * b0
    if l0 == 0:
        a = ref[:rows, base : base + LANE]
    elif l0 < LANE:
        a = pltpu.roll(ref[:rows, base : base + WIN], WIN - l0, axis=1)[:, :LANE]
    elif l0 == LANE:
        a = ref[:rows, base + LANE : base + WIN]
    else:
        a = pltpu.roll(ref[:rows, base + LANE : base + WIN], WIN - l0, axis=1)
    if n0 < LANE:
        b = pltpu.roll(ref[:rows, base + WIN : base + WIN + LANE], n0, axis=1)
        a = jnp.where(iota(a.shape, 1) < n0, a, b)
    return a


def kernel(depths, strips, vol_hbm, meas_hbm, rt_hbm, ct_hbm, pm_hbm, rad_hbm, out_hbm,
           rt_ref, ct_ref, pm_ref, rad_ref,
           v32, spr, pw, pc, sb, qb, rb, s_ref, hb, mc, rc, wr, ga, bpw,
           ctf, up, fm, gm, bt, bfm, cinv, rinv,
           sem_vol, sem_out, sem_in, sem_ms, sem_mr, sem_ps, sem_pr, sem_rs, sem_rr,
           sem_hs, sem_hr, sem_as, sem_ar, sem_fs, sem_fr):
    planes, rows, cols = vol_hbm.shape
    ext = rows + 2 * HALO
    kext = ga.shape[0]
    edge = 4 * HALO
    nk = cols // LANE
    chips = depths // 2
    d = lax.axis_index("depth")
    s = lax.axis_index("strip")
    c = lax.rem(d, 2)
    chip = d // 2
    sibling = d + 1 - 2 * c
    above = lax.rem(s + strips - 1, strips)
    below = lax.rem(s + 1, strips)
    peers = [lax.rem(chip + r, chips) for r in range(chips)]
    givers = [lax.rem(chip + chips - r, chips) for r in range(chips)]

    def strip_row(p):
        return jnp.where(p < 2 * HALO, p + rows - HALO, p - 3 * HALO)

    arg_in = []
    for i, (src, dst) in enumerate(
        ((rt_hbm, rt_ref), (ct_hbm, ct_ref), (pm_hbm, pm_ref), (rad_hbm, rad_ref))
    ):
        copy = pltpu.make_async_copy(src, dst, sem_in.at[i])
        copy.start()
        arg_in.append(copy)
    vol_in = []
    for z in range(planes):
        copy = pltpu.make_async_copy(
            vol_hbm.at[z], v32.at[z, 0:rows, LANE : LANE + cols], sem_vol.at[z]
        )
        copy.start()
        vol_in.append(copy)
    mc_in = []
    for it in range(ITERS):
        mine = CHUNKS[it][0][0] + (CHUNKS[it][1][0] - CHUNKS[it][0][0]) * c + chip
        col0 = pl.multiple_of(jnp.minimum(mine, nk - 1) * LANE, LANE)
        mc_in.append(pltpu.make_async_copy(
            meas_hbm.at[0 : rows - HALO, pl.ds(col0, LANE)],
            mc.at[it, 3 * HALO : ext, :], sem_in.at[4 + 2 * it],
        ))
        mc_in.append(pltpu.make_async_copy(
            meas_hbm.at[rows - HALO : rows, pl.ds(col0, LANE)],
            mc.at[it, 0:HALO, :], sem_in.at[5 + 2 * it],
        ))
    for copy in mc_in:
        copy.start()

    barrier = pltpu.get_barrier_semaphore()
    pl.semaphore_signal(barrier, inc=1, device_id={"depth": sibling}, device_id_type=MESH)
    for r in range(1, chips):
        pl.semaphore_signal(
            barrier, inc=1, device_id={"depth": 2 * peers[r] + c}, device_id_type=MESH
        )
    for t in (above, below):
        pl.semaphore_signal(barrier, inc=1, device_id={"strip": t}, device_id_type=MESH)

    for z in range(planes):
        v32[z, rows:, :] = jnp.zeros((LANE - rows, v32.shape[2]), F32)
        v32[z, :, 0:LANE] = jnp.zeros((LANE, LANE), F32)
        v32[z, :, LANE + cols :] = jnp.zeros((LANE, v32.shape[2] - LANE - cols), F32)
    for it in range(ITERS):
        for q in range(2):
            for k in range(CHUNKS[it][q][1], chips):
                pc[it, q, k] = jnp.zeros((ext, LANE), BF)
        rc[it, 0] = jnp.zeros((kext, LANE), BF)
        rc[it, nk + 1] = jnp.zeros((kext, LANE), BF)
        for k in range(1, nk + 1):
            rc[it, k, ext:, :] = jnp.zeros((kext - ext, LANE), BF)

    up[...] = jnp.zeros_like(up)
    every = jnp.where(lax.rem(iota((WIN, LANE), 0), PITCH) == iota((WIN, LANE), 1), 1.0, 0.0)
    every = every.astype(BF)
    y = s * rows + strip_row(iota((kext, LANE), 0))
    inside = (y >= 0) & (y < rows * strips) & (iota((kext, LANE), 0) < ext)
    inside = jnp.where(inside, 1.0, 0.0).astype(BF)
    block = iota((16, WIN), 0)
    xo = jnp.where(block < MOST, FIRST[0] + BW * block, FIRST[1] + BW * (block - MOST))
    xo = xo + iota((16, WIN), 1)
    xs = xo - RMAX
    ones_win = jnp.where((xs >= 0) & (xs < cols), 1.0, 0.0).astype(BF)
    col_ok = (xo < cols) & (iota((16, WIN), 1) < BW)
    row_ok = iota((LANE, LANE), 0) < rows
    for copy in arg_in:
        copy.wait()
    for z in range(planes):
        reach = rad_ref[z]
        ctf[...] = jnp.zeros_like(ctf)
        keep = jnp.abs(iota((PITCH, TAPS), 1) - RMAX) <= reach
        ctf[0:PITCH, 0:TAPS] = jnp.where(keep, ct_ref[:, z, :], 0.0)
        keep1 = jnp.abs(iota((1, TAPS), 1) - RMAX) <= reach
        ctf[16:17, 0:TAPS] = jnp.where(keep1, rt_ref[z : z + 1, :], 0.0)
        family = jnp.full((16, LANE), -1, jnp.int32)
        for p in range(PITCH):
            family = jnp.where(iota((16, LANE), 0) == p, pm_ref[z, p], family)
        pick = jnp.where(family == iota((16, LANE), 1), 1.0, 0.0).astype(BF)
        table = ctf[...].astype(BF)
        up[0:16, :] = dot(pick, table)
        taps = dot(every, up[...].astype(BF))
        taps = jnp.concatenate([taps, jnp.zeros((WIN, WIN - LANE), F32)], axis=1)
        fwd = pltpu.roll(taps, 32 - 2 * RMAX, axis=1)
        fwd = pltpu.roll(fwd, WIN - 32, axis=1, stride=1, stride_axis=0)
        fm[z] = fwd.astype(BF)
        back = pltpu.roll(taps, 0, axis=1, stride=1, stride_axis=0)
        gm[z] = jnp.transpose(back).astype(BF)
        rtap = jnp.concatenate([ctf[16:17, :], jnp.zeros((1, WIN - LANE), F32)], axis=1)
        rtap = jnp.broadcast_to(rtap, (LANE, WIN))
        band = pltpu.roll(rtap, 1, axis=1)
        band = pltpu.roll(band, 0, axis=1, stride=1, stride_axis=0)
        p = iota((LANE, WIN), 1)
        last = pltpu.roll(band, WIN - rows, axis=1)
        band = jnp.where(p < 2 * HALO, last, pltpu.roll(band, 2 * HALO, axis=1))
        band = jnp.where(p < ext, band, 0.0)
        bt[z] = band[:, :kext].astype(BF)
        bfm[:, LANE * z : LANE * (z + 1)] = jnp.transpose(band)[:kext, :].astype(BF)
        rn = dot(bt[z], inside)
        rinv[z] = jnp.where(row_ok, 1.0 / rn, 0.0)
        cn = dot(ones_win, gm[z])
        cinv[z] = jnp.where(col_ok, 1.0 / cn, 0.0)

    pl.semaphore_wait(barrier, chips + 2)
    for copy in mc_in:
        copy.wait()
    def m_up(it):
        return pltpu.make_async_remote_copy(
            src_ref=mc.at[it, 3 * HALO : 4 * HALO, :], dst_ref=mc.at[it, HALO : 2 * HALO, :],
            send_sem=sem_ms.at[it, 0], recv_sem=sem_mr.at[it, 0],
            device_id={"strip": above}, device_id_type=MESH,
        )

    def m_down(it):
        return pltpu.make_async_remote_copy(
            src_ref=mc.at[it, 0:HALO, :], dst_ref=mc.at[it, 2 * HALO : 3 * HALO, :],
            send_sem=sem_ms.at[it, 1], recv_sem=sem_mr.at[it, 1],
            device_id={"strip": below}, device_id_type=MESH,
        )

    for it in range(ITERS):
        m_up(it).start()
        m_down(it).start()
    for copy in vol_in:
        copy.wait()

    def groups(count):
        return [(g, min(3, count - g)) for g in range(0, count, 3)]

    def window(z, start):
        q, sh = divmod(LANE - RMAX + start, LANE)
        x = v32[z, :, LANE * q : LANE * q + WIN + LANE]
        if sh:
            x = pltpu.roll(x, WIN + LANE - sh, axis=1)
        return x[:, :WIN].astype(BF)

    def spread(it, q):
        first, count = SPREAD[it][q]
        start = FIRST[q] + BW * first

        @pl.loop(0, planes)
        def _(z):
            for g, n in groups(count):
                lhs = jnp.concatenate([window(z, start + BW * (g + i)) for i in range(n)], axis=0)
                res = dot(lhs, fm[z])
                for i in range(n):
                    spr[pl.ds(pl.multiple_of(z * LANE, LANE), LANE),
                        WIN * (g + i) : WIN * (g + i + 1)] = (
                        res[LANE * i : LANE * (i + 1)].astype(BF)
                    )

    def sensor_part(it, q):
        first, count = SPREAD[it][q]
        start = FIRST[q] + BW * first
        for b in range(count):
            pw[:, WIN * b : WIN * (b + 1)] = dot(bfm[...], spr[:, WIN * b : WIN * (b + 1)])
        base, n = CHUNKS[it][q]
        for k in range(n):
            pc[it, q, k] = unwindow(pw, base + k, ext, start).astype(BF)

    def pair(it, q):
        return pltpu.make_async_remote_copy(
            src_ref=pc.at[it, q], dst_ref=sb.at[it],
            send_sem=sem_ps.at[it], recv_sem=sem_pr.at[it],
            device_id={"depth": sibling}, device_id_type=MESH,
        )

    def part(it, r):
        return pltpu.make_async_remote_copy(
            src_ref=qb.at[it, r], dst_ref=rb.at[it, r],
            send_sem=sem_rs.at[it, r], recv_sem=sem_rr.at[it, r],
            device_id={"depth": 2 * peers[r] + c}, device_id_type=MESH,
        )

    def h_up(it):
        return pltpu.make_async_remote_copy(
            src_ref=s_ref.at[it, 2 * HALO : edge], dst_ref=hb.at[it, 0 : 2 * HALO],
            send_sem=sem_hs.at[it, 0], recv_sem=sem_hr.at[it, 0],
            device_id={"strip": above}, device_id_type=MESH,
        )

    def h_down(it):
        return pltpu.make_async_remote_copy(
            src_ref=s_ref.at[it, 0 : 2 * HALO], dst_ref=hb.at[it, 2 * HALO : edge],
            send_sem=sem_hs.at[it, 1], recv_sem=sem_hr.at[it, 1],
            device_id={"strip": below}, device_id_type=MESH,
        )

    def slot(it, q, k):
        base, n = CHUNKS[it][q]
        if n == chips:
            return 1 + base + k
        return 1 + base + k + (k // n) * (nk + 1 - base - n)

    def give(it, at, target, send, recv):
        at = rc.at[it, at, 0:ext, :]
        return pltpu.make_async_remote_copy(
            src_ref=at, dst_ref=at, send_sem=send, recv_sem=recv,
            device_id={"depth": target}, device_id_type=MESH,
        )

    def to_chip(it, q, r):
        return give(it, slot(it, q, chip), 2 * peers[r] + c, sem_as.at[it, r], sem_ar.at[it, r])

    def from_chip(it, q, r):
        return give(it, slot(it, q, givers[r]), sibling, sem_as.at[it, r], sem_ar.at[it, r])

    def to_core(it, q, r):
        return give(it, slot(it, q, givers[r]), sibling, sem_fs.at[it, r], sem_fr.at[it, r])

    def pair_send(it, q):
        @pl.when(c != q)
        def _():
            pair(it, q).start()

    def part_send(it, q):
        @pl.when(c == q)
        def _():
            pair(it, q).wait_recv()
            for r in range(1, chips):
                k = peers[r]
                qb[it, r] = (pc[it, q, k].astype(F32) + sb[it, k].astype(F32)).astype(BF)
                part(it, r).start()

    def ratio_send(it, q):
        @pl.when(c == q)
        def _():
            total = pc[it, q, chip].astype(F32) + sb[it, chip].astype(F32)
            for r in range(1, chips):
                part(it, r).wait_recv()
                total = total + rb[it, r].astype(F32)
            s_ref[it] = total
            h_up(it).start()
            h_down(it).start()
            m_up(it).wait_recv()
            m_down(it).wait_recv()
            y = s * rows + strip_row(iota((ext, LANE), 0))
            ok = (y >= 0) & (y < rows * strips) & (chip < CHUNKS[it][q][1])
            mine = slot(it, q, chip)
            ratio = jnp.where(ok[edge:], mc[it, edge:, :] / s_ref[it, edge:, :], 0.0)
            rc[it, mine, edge:ext, :] = ratio.astype(BF)
            h_up(it).wait_recv()
            h_down(it).wait_recv()
            first = iota((edge, LANE), 0) < 2 * HALO
            other = (first & (s < strips - 1)) | (~first & (s > 0))
            shared = s_ref[it, 0:edge, :] + jnp.where(other, hb[it], 0.0)
            ratio = jnp.where(ok[:edge], mc[it, 0:edge, :] / shared, 0.0)
            rc[it, mine, 0:edge, :] = ratio.astype(BF)
            for r in range(1, chips):
                to_chip(it, q, r).start()
            to_core(it, q, 0).start()

    def ratio_forward(it, q):
        @pl.when(c == q)
        def _():
            for r in range(1, chips):
                from_chip(it, q, r).wait_recv()
                to_core(it, q, r).start()

    def ratio_arrived(it, q):
        @pl.when(c != q)
        def _():
            for r in range(chips):
                to_core(it, q, r).wait_recv()

    def back(it, q):
        count = BACK[it][q]
        last = CHUNKS[it][q][0] + CHUNKS[it][q][1]
        for b in range(count):
            at, sh = divmod(LANE - RMAX + FIRST[q] + BW * b, LANE)
            pieces = [
                rc[it, at + i].astype(F32)
                if at + i <= last or q == 1 else jnp.zeros((kext, LANE), F32)
                for i in range(3)
            ]
            x = jnp.concatenate(pieces, axis=1)
            if sh:
                x = pltpu.roll(x, WIN + LANE - sh, axis=1)
            wr[kext * b : kext * (b + 1), :] = x[:, :WIN].astype(BF)
        lo = SPLIT[it] if q == 1 else 0
        hi = SPLIT[it] if q == 0 else cols

        @pl.loop(0, planes)
        def _(z):
            for g, n in groups(count):
                res = dot(wr[kext * g : kext * (g + n), :], gm[z])
                for i in range(n):
                    ga[:, WIN * (g + i) : WIN * (g + i + 1)] = (
                        res[kext * i : kext * (i + 1)].astype(BF)
                    )
            scale = jnp.concatenate([rinv[z], rinv[z]], axis=1)
            for b in range(count):
                bp = dot(bt[z], ga[:, WIN * b : WIN * (b + 1)])
                row = MOST * q + b
                bpw[:, WIN * b : WIN * (b + 1)] = bp * scale * cinv[z, row : row + 1, :]
            for k in range(lo // LANE, -(-hi // LANE)):
                at = slice(LANE * (k + 1), LANE * (k + 2))
                factor = unwindow(bpw, k, LANE, FIRST[q])
                x = iota(factor.shape, 1) + LANE * k
                if LANE * k < lo:
                    factor = jnp.where(x >= lo, factor, 1.0)
                if LANE * (k + 1) > hi:
                    factor = jnp.where(x < hi, factor, 1.0)
                v32[z, :, at] = v32[z, :, at] * factor
            if it == ITERS - 1 and q == 1:
                pltpu.make_async_copy(
                    v32.at[z, 0:rows, LANE : LANE + cols], out_hbm.at[z], sem_out.at[z]
                ).start()

    def forward(it, q):
        spread(it, q)
        if it == 0 and q == 1:
            part_send(it, 0)
        sensor_part(it, q)
        pair_send(it, q)
        if it > 0 or q == 1:
            part_send(it, q)

    forward(0, 0)
    forward(0, 1)
    for it in range(ITERS):
        ratio_send(it, 0)
        ratio_send(it, 1)
        ratio_forward(it, 0)
        ratio_arrived(it, 0)
        back(it, 0)
        ratio_forward(it, 1)
        if it + 1 < ITERS:
            forward(it + 1, 0)
        ratio_arrived(it, 1)
        back(it, 1)
        if it + 1 < ITERS:
            forward(it + 1, 1)

    for it in range(ITERS):
        m_up(it).wait_send()
        m_down(it).wait_send()
        for q in range(2):
            @pl.when(c != q)
            def _():
                pair(it, q).wait_send()

            @pl.when(c == q)
            def _():
                h_up(it).wait_send()
                h_down(it).wait_send()
                for r in range(1, chips):
                    part(it, r).wait_send()
                    to_chip(it, q, r).wait_send()
                for r in range(chips):
                    to_core(it, q, r).wait_send()
    for z in range(planes):
        pltpu.make_async_copy(
            v32.at[z, 0:rows, LANE : LANE + cols], out_hbm.at[z], sem_out.at[z]
        ).wait()


def local(depths, strips, volume, measured, row_taps, col_taps, phase_map, radius):
    planes, rows, cols = volume.shape
    ext = rows + 2 * HALO
    kext = 160
    nk = cols // LANE
    chips = depths // 2
    dma = pltpu.SemaphoreType.DMA
    vmem = pltpu.VMEM
    return pl.pallas_call(
        functools.partial(kernel, depths, strips),
        out_shape=jax.ShapeDtypeStruct(volume.shape, F32),
        in_specs=[pl.BlockSpec(memory_space=pltpu.HBM)] * 6,
        out_specs=pl.BlockSpec(memory_space=pl.ANY),
        scratch_shapes=[
            vmem(row_taps.shape, F32),
            vmem((PITCH, planes, TAPS), F32),
            pltpu.SMEM(phase_map.shape, jnp.int32),
            pltpu.SMEM(radius.shape, jnp.int32),
            vmem((planes, LANE, cols + 2 * LANE), F32),
            vmem((planes * LANE, MOST * WIN), BF),
            vmem((kext, MOST * WIN), F32),
            vmem((ITERS, 2, chips, ext, LANE), BF),
            vmem((ITERS, chips, ext, LANE), BF),
            vmem((ITERS, chips, ext, LANE), BF),
            vmem((ITERS, chips, ext, LANE), BF),
            vmem((ITERS, ext, LANE), F32),
            vmem((ITERS, 4 * HALO, LANE), F32),
            vmem((ITERS, ext, LANE), F32),
            vmem((ITERS, nk + 3, kext, LANE), BF),
            vmem((MOST * kext, WIN), BF),
            vmem((kext, MOST * WIN), BF),
            vmem((LANE, MOST * WIN), F32),
            vmem((LANE, LANE), F32),
            vmem((LANE, LANE), F32),
            vmem((planes, WIN, WIN), BF),
            vmem((planes, WIN, WIN), BF),
            vmem((planes, LANE, kext), BF),
            vmem((kext, planes * LANE), BF),
            vmem((planes, 16, WIN), F32),
            vmem((planes, LANE, LANE), F32),
            dma((planes,)),
            dma((planes,)),
            dma((4 + 2 * ITERS,)),
            dma((ITERS, 2)),
            dma((ITERS, 2)),
            dma((ITERS,)),
            dma((ITERS,)),
            dma((ITERS, chips)),
            dma((ITERS, chips)),
            dma((ITERS, 2)),
            dma((ITERS, 2)),
            dma((ITERS, chips)),
            dma((ITERS, chips)),
            dma((ITERS, chips)),
            dma((ITERS, chips)),
        ],
        compiler_params=pltpu.CompilerParams(
            collective_id=0, has_side_effects=True, vmem_limit_bytes=48 * 1024 * 1024
        ),
    )(*(
        pltpu.with_memory_space_constraint(x, pltpu.HBM)
        for x in (volume, measured, row_taps, jnp.transpose(col_taps, (1, 0, 2)), phase_map, radius)
    ))


def solution(mesh):
    return jax.shard_map(
        functools.partial(local, mesh.shape["depth"], mesh.shape["strip"]),
        mesh=mesh,
        in_specs=(
            P("depth", "strip", None),
            P("strip", None),
            P("depth", None),
            P("depth", None, None),
            P("depth", None),
            P("depth"),
        ),
        out_specs=P("depth", "strip", None),
        check_vma=False,
    )
```

```python
import functools

import jax
import jax.numpy as jnp
from jax import lax
from jax.experimental import pallas as pl
from jax.experimental.pallas import tpu as pltpu
from jax.sharding import PartitionSpec as P

PITCH = 15
RMAX = 15
TAPS = 2 * RMAX + 1
ITERS = 2
LANE = 128
WIN = 256
BW = 225
FIRST = (0, 795)
SPREAD = (((0, 5), (1, 4)), ((0, 4), (0, 5)))
CHUNKS = (((0, 8), (8, 7)), ((0, 7), (7, 8)))
BACK = ((5, 5), (4, 5))
SPLIT = (1005, 870)
MOST = 5
HALO = 16
MESH = pl.DeviceIdType.MESH
BF = jnp.bfloat16
F32 = jnp.float32


def iota(shape, axis):
    return lax.broadcasted_iota(jnp.int32, shape, axis)


def dot(a, b):
    return jnp.dot(a, b, preferred_element_type=F32)


def unwindow(ref, k, rows, start):
    b0, l0 = divmod(LANE * k - start, BW)
    if b0 < 0:
        return pltpu.roll(ref[:rows, 0:LANE], start - LANE * k, axis=1)
    n0 = min(LANE, BW - l0)
    base = WIN * b0
    if l0 == 0:
        a = ref[:rows, base : base + LANE]
    elif l0 < LANE:
        a = pltpu.roll(ref[:rows, base : base + WIN], WIN - l0, axis=1)[:, :LANE]
    elif l0 == LANE:
        a = ref[:rows, base + LANE : base + WIN]
    else:
        a = pltpu.roll(ref[:rows, base + LANE : base + WIN], WIN - l0, axis=1)
    if n0 < LANE:
        b = pltpu.roll(ref[:rows, base + WIN : base + WIN + LANE], n0, axis=1)
        a = jnp.where(iota(a.shape, 1) < n0, a, b)
    return a


def kernel(depths, strips, vol_hbm, meas_hbm, rt_hbm, ct_hbm, pm_hbm, rad_hbm, out_hbm,
           rt_ref, ct_ref, pm_ref, rad_ref,
           v32, spr, pw, pc, sb, qb, rb, ub, mc, rc, wr, ga, bpw,
           ctf, up, fm, gm, bt, bfm, cinv, rinv,
           sem_vol, sem_out, sem_in, sem_ms, sem_mr, sem_ps, sem_pr, sem_rs, sem_rr,
           sem_hs, sem_hr, sem_as, sem_ar, sem_fs, sem_fr):
    planes, rows, cols = vol_hbm.shape
    ext = rows + 2 * HALO
    kext = ga.shape[1]
    edge = 4 * HALO
    nk = cols // LANE
    chips = depths // 2
    d = lax.axis_index("depth")
    s = lax.axis_index("strip")
    c = lax.rem(d, 2)
    chip = d // 2
    sibling = d + 1 - 2 * c
    above = lax.rem(s + strips - 1, strips)
    below = lax.rem(s + 1, strips)
    ys = chips // 2
    xc, yc = chip // ys, lax.rem(chip, ys)
    peers = [lax.rem(xc + r // ys, 2) * ys + lax.rem(yc + r, ys) for r in range(chips)]
    givers = [lax.rem(xc + r // ys, 2) * ys + lax.rem(yc + ys - r % ys, ys) for r in range(chips)]
    near = sorted(range(1, chips), key=lambda r: 2 * (r // ys) + min(r % ys, ys - r % ys))
    far = near[::-1]

    def strip_row(p):
        return jnp.where(p < 2 * HALO, p + rows - HALO, p - 3 * HALO)

    arg_in = []
    for i, (src, dst) in enumerate(
        ((rt_hbm, rt_ref), (ct_hbm, ct_ref), (pm_hbm, pm_ref), (rad_hbm, rad_ref))
    ):
        copy = pltpu.make_async_copy(src, dst, sem_in.at[i])
        copy.start()
        arg_in.append(copy)
    vol_in = []
    for z in range(planes):
        copy = pltpu.make_async_copy(
            vol_hbm.at[z], v32.at[z, 0:rows, LANE : LANE + cols], sem_vol.at[z]
        )
        copy.start()
        vol_in.append(copy)
    mc_in = []
    for it in range(ITERS):
        mine = CHUNKS[it][0][0] + (CHUNKS[it][1][0] - CHUNKS[it][0][0]) * c + chip
        col0 = pl.multiple_of(jnp.minimum(mine, nk - 1) * LANE, LANE)
        mc_in.append(pltpu.make_async_copy(
            meas_hbm.at[0 : rows - HALO, pl.ds(col0, LANE)],
            mc.at[it, 3 * HALO : ext, :], sem_in.at[4 + 2 * it],
        ))
        mc_in.append(pltpu.make_async_copy(
            meas_hbm.at[rows - HALO : rows, pl.ds(col0, LANE)],
            mc.at[it, 0:HALO, :], sem_in.at[5 + 2 * it],
        ))
    for copy in mc_in:
        copy.start()

    barrier = pltpu.get_barrier_semaphore()
    pl.semaphore_signal(barrier, inc=1, device_id={"depth": sibling}, device_id_type=MESH)
    for r in range(1, chips):
        pl.semaphore_signal(
            barrier, inc=1, device_id={"depth": 2 * peers[r] + c}, device_id_type=MESH
        )
    for t in (above, below):
        for r in range(chips):
            pl.semaphore_signal(
                barrier, inc=1, device_id={"depth": 2 * peers[r] + c, "strip": t},
                device_id_type=MESH,
            )

    for z in range(planes):
        v32[z, rows:, :] = jnp.zeros((LANE - rows, v32.shape[2]), F32)
        v32[z, :, 0:LANE] = jnp.zeros((LANE, LANE), F32)
        v32[z, :, LANE + cols :] = jnp.zeros((LANE, v32.shape[2] - LANE - cols), F32)
    for it in range(ITERS):
        for q in range(2):
            for k in range(CHUNKS[it][q][1], chips):
                pc[it, q, k] = jnp.zeros((ext, LANE), BF)
        rc[it, 0] = jnp.zeros((kext, LANE), BF)
        rc[it, nk + 1] = jnp.zeros((kext, LANE), BF)
        for k in range(1, nk + 1):
            rc[it, k, ext:, :] = jnp.zeros((kext - ext, LANE), BF)

    up[...] = jnp.zeros_like(up)
    every = jnp.where(lax.rem(iota((WIN, LANE), 0), PITCH) == iota((WIN, LANE), 1), 1.0, 0.0)
    every = every.astype(BF)
    y = s * rows + strip_row(iota((kext, LANE), 0))
    inside = (y >= 0) & (y < rows * strips) & (iota((kext, LANE), 0) < ext)
    inside = jnp.where(inside, 1.0, 0.0).astype(BF)
    block = iota((16, WIN), 0)
    xo = jnp.where(block < MOST, FIRST[0] + BW * block, FIRST[1] + BW * (block - MOST))
    xo = xo + iota((16, WIN), 1)
    xs = xo - RMAX
    ones_win = jnp.where((xs >= 0) & (xs < cols), 1.0, 0.0).astype(BF)
    col_ok = (xo < cols) & (iota((16, WIN), 1) < BW)
    row_ok = iota((LANE, LANE), 0) < rows
    for copy in arg_in:
        copy.wait()
    for z in range(planes):
        reach = rad_ref[z]
        ctf[...] = jnp.zeros_like(ctf)
        keep = jnp.abs(iota((PITCH, TAPS), 1) - RMAX) <= reach
        ctf[0:PITCH, 0:TAPS] = jnp.where(keep, ct_ref[:, z, :], 0.0)
        keep1 = jnp.abs(iota((1, TAPS), 1) - RMAX) <= reach
        ctf[16:17, 0:TAPS] = jnp.where(keep1, rt_ref[z : z + 1, :], 0.0)
        family = jnp.full((16, LANE), -1, jnp.int32)
        for p in range(PITCH):
            family = jnp.where(iota((16, LANE), 0) == p, pm_ref[z, p], family)
        pick = jnp.where(family == iota((16, LANE), 1), 1.0, 0.0).astype(BF)
        table = ctf[...].astype(BF)
        up[0:16, :] = dot(pick, table)
        taps = dot(every, up[...].astype(BF))
        taps = jnp.concatenate([taps, jnp.zeros((WIN, WIN - LANE), F32)], axis=1)
        fwd = pltpu.roll(taps, 32 - 2 * RMAX, axis=1)
        fwd = pltpu.roll(fwd, WIN - 32, axis=1, stride=1, stride_axis=0)
        fm[z] = fwd.astype(BF)
        back = pltpu.roll(taps, 0, axis=1, stride=1, stride_axis=0)
        gm[z] = jnp.transpose(back).astype(BF)
        rtap = jnp.concatenate([ctf[16:17, :], jnp.zeros((1, WIN - LANE), F32)], axis=1)
        rtap = jnp.broadcast_to(rtap, (LANE, WIN))
        band = pltpu.roll(rtap, 1, axis=1)
        band = pltpu.roll(band, 0, axis=1, stride=1, stride_axis=0)
        p = iota((LANE, WIN), 1)
        last = pltpu.roll(band, WIN - rows, axis=1)
        band = jnp.where(p < 2 * HALO, last, pltpu.roll(band, 2 * HALO, axis=1))
        band = jnp.where(p < ext, band, 0.0)
        bt[z] = band[:, :kext].astype(BF)
        bfm[:, LANE * z : LANE * (z + 1)] = jnp.transpose(band)[:kext, :].astype(BF)
        rn = dot(bt[z], inside)
        rinv[z] = jnp.where(row_ok, 1.0 / rn, 0.0)
        cn = dot(ones_win, gm[z])
        cinv[z] = jnp.where(col_ok, 1.0 / cn, 0.0)

    pl.semaphore_wait(barrier, 3 * chips)
    for copy in mc_in:
        copy.wait()
    def m_up(it):
        return pltpu.make_async_remote_copy(
            src_ref=mc.at[it, 3 * HALO : 4 * HALO, :], dst_ref=mc.at[it, HALO : 2 * HALO, :],
            send_sem=sem_ms.at[it, 0], recv_sem=sem_mr.at[it, 0],
            device_id={"strip": above}, device_id_type=MESH,
        )

    def m_down(it):
        return pltpu.make_async_remote_copy(
            src_ref=mc.at[it, 0:HALO, :], dst_ref=mc.at[it, 2 * HALO : 3 * HALO, :],
            send_sem=sem_ms.at[it, 1], recv_sem=sem_mr.at[it, 1],
            device_id={"strip": below}, device_id_type=MESH,
        )

    for it in range(ITERS):
        m_up(it).start()
        m_down(it).start()
    for copy in vol_in:
        copy.wait()

    def groups(count):
        return [(g, min(3, count - g)) for g in range(0, count, 3)]

    def window(z, start):
        q, sh = divmod(LANE - RMAX + start, LANE)
        x = v32[z, :, LANE * q : LANE * q + WIN + LANE]
        if sh:
            x = pltpu.roll(x, WIN + LANE - sh, axis=1)
        return x[:, :WIN].astype(BF)

    def spread(it, q):
        first, count = SPREAD[it][q]
        start = FIRST[q] + BW * first

        for z in range(planes):
            for g, n in groups(count):
                lhs = jnp.concatenate([window(z, start + BW * (g + i)) for i in range(n)], axis=0)
                res = dot(lhs, fm[z])
                for i in range(n):
                    spr[z * LANE : (z + 1) * LANE,
                        WIN * (g + i) : WIN * (g + i + 1)] = (
                        res[LANE * i : LANE * (i + 1)].astype(BF)
                    )

    def sensor_part(it, q):
        first, count = SPREAD[it][q]
        start = FIRST[q] + BW * first
        for b in range(count):
            pw[:, WIN * b : WIN * (b + 1)] = dot(bfm[...], spr[:, WIN * b : WIN * (b + 1)])
        base, n = CHUNKS[it][q]
        for k in range(n):
            pc[it, q, k] = unwindow(pw, base + k, ext, start).astype(BF)

    def pair(it, q):
        return pltpu.make_async_remote_copy(
            src_ref=pc.at[it, q], dst_ref=sb.at[it],
            send_sem=sem_ps.at[it], recv_sem=sem_pr.at[it],
            device_id={"depth": sibling}, device_id_type=MESH,
        )

    def part(it, r):
        return pltpu.make_async_remote_copy(
            src_ref=qb.at[it, r], dst_ref=rb.at[it, r],
            send_sem=sem_rs.at[it, r], recv_sem=sem_rr.at[it, r],
            device_id={"depth": 2 * peers[r] + c}, device_id_type=MESH,
        )

    def shared_part(it, side, r):
        at = slice(2 * HALO, edge) if side == 0 else slice(0, 2 * HALO)
        return pltpu.make_async_remote_copy(
            src_ref=qb.at[it, r, at, :], dst_ref=ub.at[it, side, r],
            send_sem=sem_hs.at[it, side], recv_sem=sem_hr.at[it, side],
            device_id={"depth": 2 * peers[r] + c, "strip": (above, below)[side]},
            device_id_type=MESH,
        )

    def all_shared(it, side):
        return pltpu.make_async_remote_copy(
            src_ref=ub.at[it, side], dst_ref=ub.at[it, side],
            send_sem=sem_hs.at[it, side], recv_sem=sem_hr.at[it, side],
            device_id={"strip": (above, below)[side]}, device_id_type=MESH,
        )

    def slot(it, q, k):
        base, n = CHUNKS[it][q]
        if n == chips:
            return 1 + base + k
        return 1 + base + k + (k // n) * (nk + 1 - base - n)

    def give(it, at, target, send, recv):
        at = rc.at[it, at, 0:ext, :]
        return pltpu.make_async_remote_copy(
            src_ref=at, dst_ref=at, send_sem=send, recv_sem=recv,
            device_id={"depth": target}, device_id_type=MESH,
        )

    def to_chip(it, q, r):
        return give(it, slot(it, q, chip), 2 * peers[r] + c, sem_as.at[it, r], sem_ar.at[it, r])

    def from_chip(it, q, r):
        return give(it, slot(it, q, givers[r]), sibling, sem_as.at[it, r], sem_ar.at[it, r])

    def to_core(it, q, r):
        return give(it, slot(it, q, givers[r]), sibling, sem_fs.at[it, r], sem_fr.at[it, r])

    def pair_send(it, q):
        @pl.when(c != q)
        def _():
            pair(it, q).start()

    def part_send(it, q):
        @pl.when(c == q)
        def _():
            pair(it, q).wait_recv()
            for r in far + [0]:
                k = peers[r]
                qb[it, r] = (pc[it, q, k].astype(F32) + sb[it, k].astype(F32)).astype(BF)
                shared_part(it, 0, r).start()
                shared_part(it, 1, r).start()
                if r:
                    part(it, r).start()

    def ratio_send(it, q):
        @pl.when(c == q)
        def _():
            total = pc[it, q, chip].astype(F32) + sb[it, chip].astype(F32)
            for r in near:
                part(it, r).wait_recv()
                total = total + rb[it, r].astype(F32)
            m_up(it).wait_recv()
            m_down(it).wait_recv()
            all_shared(it, 0).wait_recv()
            all_shared(it, 1).wait_recv()
            shared = [ub[it, side, 0].astype(F32) for side in range(2)]
            for r in range(1, chips):
                shared = [shared[side] + ub[it, side, r].astype(F32) for side in range(2)]
            total = jnp.concatenate([
                total[0 : 2 * HALO] + jnp.where(s < strips - 1, shared[0], 0.0),
                total[2 * HALO : edge] + jnp.where(s > 0, shared[1], 0.0),
                total[edge:],
            ], axis=0)
            y = s * rows + strip_row(iota((ext, LANE), 0))
            ok = (y >= 0) & (y < rows * strips) & (chip < CHUNKS[it][q][1])
            mine = slot(it, q, chip)
            rc[it, mine, 0:ext, :] = jnp.where(ok, mc[it] / total, 0.0).astype(BF)
            for r in far:
                to_chip(it, q, r).start()
            to_core(it, q, 0).start()

    def ratio_forward(it, q):
        @pl.when(c == q)
        def _():
            for r in near:
                from_chip(it, q, r).wait_recv()
                to_core(it, q, r).start()

    def ratio_arrived(it, q):
        @pl.when(c != q)
        def _():
            for r in range(chips):
                to_core(it, q, r).wait_recv()

    def back(it, q):
        count = BACK[it][q]
        last = CHUNKS[it][q][0] + CHUNKS[it][q][1]
        for b in range(count):
            at, sh = divmod(LANE - RMAX + FIRST[q] + BW * b, LANE)
            pieces = [
                rc[it, at + i].astype(F32)
                if at + i <= last or q == 1 else jnp.zeros((kext, LANE), F32)
                for i in range(3)
            ]
            x = jnp.concatenate(pieces, axis=1)
            if sh:
                x = pltpu.roll(x, WIN + LANE - sh, axis=1)
            wr[kext * b : kext * (b + 1), :] = x[:, :WIN].astype(BF)
        lo = SPLIT[it] if q == 1 else 0
        hi = SPLIT[it] if q == 0 else cols

        for z in range(planes):
            for g, n in groups(count):
                res = dot(wr[kext * g : kext * (g + n), :], gm[z])
                for i in range(n):
                    ga[z % 2, :, WIN * (g + i) : WIN * (g + i + 1)] = (
                        res[kext * i : kext * (i + 1)].astype(BF)
                    )
            scale = jnp.concatenate([rinv[z], rinv[z]], axis=1)
            for b in range(count):
                bp = dot(bt[z], ga[z % 2, :, WIN * b : WIN * (b + 1)])
                row = MOST * q + b
                bpw[z % 2, :, WIN * b : WIN * (b + 1)] = bp * scale * cinv[z, row : row + 1, :]
            for k in range(lo // LANE, -(-hi // LANE)):
                at = slice(LANE * (k + 1), LANE * (k + 2))
                factor = unwindow(bpw.at[z % 2], k, LANE, FIRST[q])
                x = iota(factor.shape, 1) + LANE * k
                if LANE * k < lo:
                    factor = jnp.where(x >= lo, factor, 1.0)
                if LANE * (k + 1) > hi:
                    factor = jnp.where(x < hi, factor, 1.0)
                v32[z, :, at] = v32[z, :, at] * factor
            if it == ITERS - 1 and q == 1:
                pltpu.make_async_copy(
                    v32.at[z, 0:rows, LANE : LANE + cols], out_hbm.at[z], sem_out.at[z]
                ).start()

    def forward(it, q):
        spread(it, q)
        if it == 0 and q == 1:
            part_send(it, 0)
        sensor_part(it, q)
        pair_send(it, q)
        if it > 0 or q == 1:
            part_send(it, q)

    forward(0, 0)
    forward(0, 1)
    for it in range(ITERS):
        ratio_send(it, 0)
        ratio_send(it, 1)
        ratio_forward(it, 0)
        ratio_arrived(it, 0)
        back(it, 0)
        ratio_forward(it, 1)
        if it + 1 < ITERS:
            forward(it + 1, 0)
        ratio_arrived(it, 1)
        back(it, 1)
        if it + 1 < ITERS:
            forward(it + 1, 1)

    for it in range(ITERS):
        m_up(it).wait_send()
        m_down(it).wait_send()
        for q in range(2):
            @pl.when(c != q)
            def _():
                pair(it, q).wait_send()

            @pl.when(c == q)
            def _():
                all_shared(it, 0).wait_send()
                all_shared(it, 1).wait_send()
                for r in range(1, chips):
                    part(it, r).wait_send()
                    to_chip(it, q, r).wait_send()
                for r in range(chips):
                    to_core(it, q, r).wait_send()
    for z in range(planes):
        pltpu.make_async_copy(
            v32.at[z, 0:rows, LANE : LANE + cols], out_hbm.at[z], sem_out.at[z]
        ).wait()


def local(depths, strips, volume, measured, row_taps, col_taps, phase_map, radius):
    planes, rows, cols = volume.shape
    ext = rows + 2 * HALO
    kext = 160
    nk = cols // LANE
    chips = depths // 2
    dma = pltpu.SemaphoreType.DMA
    vmem = pltpu.VMEM
    return pl.pallas_call(
        functools.partial(kernel, depths, strips),
        out_shape=jax.ShapeDtypeStruct(volume.shape, F32),
        in_specs=[pl.BlockSpec(memory_space=pltpu.HBM)] * 6,
        out_specs=pl.BlockSpec(memory_space=pl.ANY),
        scratch_shapes=[
            vmem(row_taps.shape, F32),
            vmem((PITCH, planes, TAPS), F32),
            pltpu.SMEM(phase_map.shape, jnp.int32),
            pltpu.SMEM(radius.shape, jnp.int32),
            vmem((planes, LANE, cols + 2 * LANE), F32),
            vmem((planes * LANE, MOST * WIN), BF),
            vmem((kext, MOST * WIN), F32),
            vmem((ITERS, 2, chips, ext, LANE), BF),
            vmem((ITERS, chips, ext, LANE), BF),
            vmem((ITERS, chips, ext, LANE), BF),
            vmem((ITERS, chips, ext, LANE), BF),
            vmem((ITERS, 2, chips, 2 * HALO, LANE), BF),
            vmem((ITERS, ext, LANE), F32),
            vmem((ITERS, nk + 3, kext, LANE), BF),
            vmem((MOST * kext, WIN), BF),
            vmem((2, kext, MOST * WIN), BF),
            vmem((2, LANE, MOST * WIN), F32),
            vmem((LANE, LANE), F32),
            vmem((LANE, LANE), F32),
            vmem((planes, WIN, WIN), BF),
            vmem((planes, WIN, WIN), BF),
            vmem((planes, LANE, kext), BF),
            vmem((kext, planes * LANE), BF),
            vmem((planes, 16, WIN), F32),
            vmem((planes, LANE, LANE), F32),
            dma((planes,)),
            dma((planes,)),
            dma((4 + 2 * ITERS,)),
            dma((ITERS, 2)),
            dma((ITERS, 2)),
            dma((ITERS,)),
            dma((ITERS,)),
            dma((ITERS, chips)),
            dma((ITERS, chips)),
            dma((ITERS, 2)),
            dma((ITERS, 2)),
            dma((ITERS, chips)),
            dma((ITERS, chips)),
            dma((ITERS, chips)),
            dma((ITERS, chips)),
        ],
        compiler_params=pltpu.CompilerParams(
            collective_id=0, has_side_effects=True, vmem_limit_bytes=48 * 1024 * 1024
        ),
    )(*(
        pltpu.with_memory_space_constraint(x, pltpu.HBM)
        for x in (volume, measured, row_taps, jnp.transpose(col_taps, (1, 0, 2)), phase_map, radius)
    ))


def solution(mesh):
    return jax.shard_map(
        functools.partial(local, mesh.shape["depth"], mesh.shape["strip"]),
        mesh=mesh,
        in_specs=(
            P("depth", "strip", None),
            P("strip", None),
            P("depth", None),
            P("depth", None, None),
            P("depth", None),
            P("depth"),
        ),
        out_specs=P("depth", "strip", None),
        check_vma=False,
    )
```

```python
import functools

import jax
import jax.numpy as jnp
from jax import lax
from jax.experimental import pallas as pl
from jax.experimental.pallas import tpu as pltpu
from jax.sharding import PartitionSpec as P

PITCH = 15
RMAX = 15
TAPS = 2 * RMAX + 1
ITERS = 2
LANE = 128
WIN = 256
BW = 225
FIRST = (0, 795)
SPREAD = (((0, 5), (1, 4)), ((0, 4), (0, 5)))
CHUNKS = (((0, 8), (8, 7)), ((0, 7), (7, 8)))
BACK = ((5, 5), (4, 5))
SPLIT = (1005, 870)
MOST = 5
HALO = 16
MESH = pl.DeviceIdType.MESH
BF = jnp.bfloat16
F32 = jnp.float32


def iota(shape, axis):
    return lax.broadcasted_iota(jnp.int32, shape, axis)


def dot(a, b):
    return jnp.dot(a, b, preferred_element_type=F32)


def unwindow(ref, k, rows, start):
    b0, l0 = divmod(LANE * k - start, BW)
    if b0 < 0:
        return pltpu.roll(ref[:rows, 0:LANE], start - LANE * k, axis=1)
    n0 = min(LANE, BW - l0)
    base = WIN * b0
    if l0 == 0:
        a = ref[:rows, base : base + LANE]
    elif l0 < LANE:
        a = pltpu.roll(ref[:rows, base : base + WIN], WIN - l0, axis=1)[:, :LANE]
    elif l0 == LANE:
        a = ref[:rows, base + LANE : base + WIN]
    else:
        a = pltpu.roll(ref[:rows, base + LANE : base + WIN], WIN - l0, axis=1)
    if n0 < LANE:
        b = pltpu.roll(ref[:rows, base + WIN : base + WIN + LANE], n0, axis=1)
        a = jnp.where(iota(a.shape, 1) < n0, a, b)
    return a


def kernel(depths, strips, vol_hbm, meas_hbm, rt_hbm, ct_hbm, pm_hbm, rad_hbm, out_hbm,
           rt_ref, ct_ref, pm_ref, rad_ref,
           v32, spr, pw, pc, sb, qb, rb, ub, mc, rc, wr, ga, bpw,
           ctf, up, tap_ref, fm, gm, bt, bfm, cinv, rinv,
           sem_vol, sem_out, sem_in, sem_ms, sem_mr, sem_ps, sem_pr, sem_rs, sem_rr,
           sem_hs, sem_hr, sem_as, sem_ar, sem_fs, sem_fr):
    planes, rows, cols = vol_hbm.shape
    ext = rows + 2 * HALO
    kext = ga.shape[1]
    edge = 4 * HALO
    nk = cols // LANE
    chips = depths // 2
    d = lax.axis_index("depth")
    s = lax.axis_index("strip")
    c = lax.rem(d, 2)
    chip = d // 2
    sibling = d + 1 - 2 * c
    above = lax.rem(s + strips - 1, strips)
    below = lax.rem(s + 1, strips)
    ys = chips // 2
    xc, yc = chip // ys, lax.rem(chip, ys)
    peers = [lax.rem(xc + r // ys, 2) * ys + lax.rem(yc + r, ys) for r in range(chips)]
    givers = [lax.rem(xc + r // ys, 2) * ys + lax.rem(yc + ys - r % ys, ys) for r in range(chips)]
    near = sorted(range(1, chips), key=lambda r: 2 * (r // ys) + min(r % ys, ys - r % ys))
    far = near[::-1]

    barrier = pltpu.get_barrier_semaphore()
    pl.semaphore_signal(barrier, inc=1, device_id={"depth": sibling}, device_id_type=MESH)
    for r in range(1, chips):
        pl.semaphore_signal(
            barrier, inc=1, device_id={"depth": 2 * peers[r] + c}, device_id_type=MESH
        )
    for t in (above, below):
        for r in range(chips):
            pl.semaphore_signal(
                barrier, inc=1, device_id={"depth": 2 * peers[r] + c, "strip": t},
                device_id_type=MESH,
            )

    def strip_row(p):
        return jnp.where(p < 2 * HALO, p + rows - HALO, p - 3 * HALO)

    arg_in = []
    for i, (src, dst) in enumerate(
        ((rt_hbm, rt_ref), (ct_hbm, ct_ref), (pm_hbm, pm_ref), (rad_hbm, rad_ref))
    ):
        copy = pltpu.make_async_copy(src, dst, sem_in.at[i])
        copy.start()
        arg_in.append(copy)
    def vol_in(z):
        return pltpu.make_async_copy(
            vol_hbm.at[z], v32.at[z, 0:rows, LANE : LANE + cols], sem_vol.at[z]
        )

    def vol_out(z):
        return pltpu.make_async_copy(
            v32.at[z, 0:rows, LANE : LANE + cols], out_hbm.at[z], sem_out.at[z]
        )

    for z in range(planes):
        vol_in(z).start()
    mc_in = []
    for it in range(ITERS):
        mine = CHUNKS[it][0][0] + (CHUNKS[it][1][0] - CHUNKS[it][0][0]) * c + chip
        col0 = pl.multiple_of(jnp.minimum(mine, nk - 1) * LANE, LANE)
        mc_in.append(pltpu.make_async_copy(
            meas_hbm.at[0 : rows - HALO, pl.ds(col0, LANE)],
            mc.at[it, 3 * HALO : ext, :], sem_in.at[4 + 2 * it],
        ))
        mc_in.append(pltpu.make_async_copy(
            meas_hbm.at[rows - HALO : rows, pl.ds(col0, LANE)],
            mc.at[it, 0:HALO, :], sem_in.at[5 + 2 * it],
        ))
    for copy in mc_in:
        copy.start()

    for z in range(planes):
        v32[z, rows:, :] = jnp.zeros((LANE - rows, v32.shape[2]), F32)
        v32[z, :, 0:LANE] = jnp.zeros((LANE, LANE), F32)
        v32[z, :, LANE + cols :] = jnp.zeros((LANE, v32.shape[2] - LANE - cols), F32)
    for it in range(ITERS):
        for q in range(2):
            for k in range(CHUNKS[it][q][1], chips):
                pc[it, q, k] = jnp.zeros((ext, LANE), BF)
        rc[it, 0] = jnp.zeros((kext, LANE), BF)
        rc[it, nk + 1] = jnp.zeros((kext, LANE), BF)
        for k in range(1, nk + 1):
            rc[it, k, ext:, :] = jnp.zeros((kext - ext, LANE), BF)

    up[...] = jnp.zeros_like(up)
    ctf[...] = jnp.zeros_like(ctf)
    every = jnp.where(lax.rem(iota((WIN, LANE), 0), PITCH) == iota((WIN, LANE), 1), 1.0, 0.0)
    every = every.astype(BF)
    for copy in arg_in:
        copy.wait()
    for z in range(planes):
        reach = rad_ref[z]
        keep = jnp.abs(iota((PITCH, TAPS), 1) - RMAX) <= reach
        ctf[z, 0:PITCH, 0:TAPS] = jnp.where(keep, ct_ref[:, z, :], 0.0)
        keep1 = jnp.abs(iota((1, TAPS), 1) - RMAX) <= reach
        ctf[z, 16:17, 0:TAPS] = jnp.where(keep1, rt_ref[z : z + 1, :], 0.0)
        family = jnp.full((16, LANE), -1, jnp.int32)
        for p in range(PITCH):
            family = jnp.where(iota((16, LANE), 0) == p, pm_ref[z, p], family)
        pick = jnp.where(family == iota((16, LANE), 1), 1.0, 0.0).astype(BF)
        table = ctf[z].astype(BF)
        up[z, 0:16, :] = dot(pick, table)
        taps = dot(every, up[z].astype(BF))
        tap_ref[z] = taps
        taps = jnp.concatenate([taps, jnp.zeros((WIN, WIN - LANE), F32)], axis=1)
        fwd = pltpu.roll(taps, 32 - 2 * RMAX, axis=1)
        fwd = pltpu.roll(fwd, WIN - 32, axis=1, stride=1, stride_axis=0)
        fm[z] = fwd.astype(BF)
        rtap = jnp.concatenate([ctf[z, 16:17, :], jnp.zeros((1, WIN - LANE), F32)], axis=1)
        rtap = jnp.broadcast_to(rtap, (LANE, WIN))
        band = pltpu.roll(rtap, 1, axis=1)
        band = pltpu.roll(band, 0, axis=1, stride=1, stride_axis=0)
        p = iota((LANE, WIN), 1)
        last = pltpu.roll(band, WIN - rows, axis=1)
        band = jnp.where(p < 2 * HALO, last, pltpu.roll(band, 2 * HALO, axis=1))
        band = jnp.where(p < ext, band, 0.0)
        bt[z] = band[:, :kext].astype(BF)
        bfm[:, LANE * z : LANE * (z + 1)] = jnp.transpose(band)[:kext, :].astype(BF)

    def back_operators():
        y = s * rows + strip_row(iota((kext, LANE), 0))
        inside = (y >= 0) & (y < rows * strips) & (iota((kext, LANE), 0) < ext)
        inside = jnp.where(inside, 1.0, 0.0).astype(BF)
        block = iota((16, WIN), 0)
        xo = jnp.where(block < MOST, FIRST[0] + BW * block, FIRST[1] + BW * (block - MOST))
        xo = xo + iota((16, WIN), 1)
        xs = xo - RMAX
        ones_win = jnp.where((xs >= 0) & (xs < cols), 1.0, 0.0).astype(BF)
        col_ok = (xo < cols) & (iota((16, WIN), 1) < BW)
        row_ok = iota((LANE, LANE), 0) < rows
        for z in range(planes):
            taps = jnp.concatenate([tap_ref[z], jnp.zeros((WIN, WIN - LANE), F32)], axis=1)
            taps = pltpu.roll(taps, 0, axis=1, stride=1, stride_axis=0)
            gm[z] = jnp.transpose(taps).astype(BF)
            rn = dot(bt[z], inside)
            rinv[z] = jnp.where(row_ok, 1.0 / rn, 0.0)
            cn = dot(ones_win, gm[z])
            cinv[z] = jnp.where(col_ok, 1.0 / cn, 0.0)

    def m_up(it):
        return pltpu.make_async_remote_copy(
            src_ref=mc.at[it, 3 * HALO : 4 * HALO, :], dst_ref=mc.at[it, HALO : 2 * HALO, :],
            send_sem=sem_ms.at[it, 0], recv_sem=sem_mr.at[it, 0],
            device_id={"strip": above}, device_id_type=MESH,
        )

    def m_down(it):
        return pltpu.make_async_remote_copy(
            src_ref=mc.at[it, 0:HALO, :], dst_ref=mc.at[it, 2 * HALO : 3 * HALO, :],
            send_sem=sem_ms.at[it, 1], recv_sem=sem_mr.at[it, 1],
            device_id={"strip": below}, device_id_type=MESH,
        )

    def meet():
        pl.semaphore_wait(barrier, 3 * chips)
        for copy in mc_in:
            copy.wait()
        for it in range(ITERS):
            m_up(it).start()
            m_down(it).start()

    def groups(count):
        return [(g, min(3, count - g)) for g in range(0, count, 3)]

    def window(z, start):
        q, sh = divmod(LANE - RMAX + start, LANE)
        x = v32[z, :, LANE * q : LANE * q + WIN + LANE]
        if sh:
            x = pltpu.roll(x, WIN + LANE - sh, axis=1)
        return x[:, :WIN].astype(BF)

    def spread(it, q):
        first, count = SPREAD[it][q]
        start = FIRST[q] + BW * first

        for z in range(planes):
            if it == 0 and q == 0:
                vol_in(z).wait()
            for g, n in groups(count):
                lhs = jnp.concatenate([window(z, start + BW * (g + i)) for i in range(n)], axis=0)
                res = dot(lhs, fm[z])
                for i in range(n):
                    spr[z * LANE : (z + 1) * LANE,
                        WIN * (g + i) : WIN * (g + i + 1)] = (
                        res[LANE * i : LANE * (i + 1)].astype(BF)
                    )

    def sensor_part(it, q):
        first, count = SPREAD[it][q]
        start = FIRST[q] + BW * first
        for b in range(count):
            pw[:, WIN * b : WIN * (b + 1)] = dot(bfm[...], spr[:, WIN * b : WIN * (b + 1)])
        base, n = CHUNKS[it][q]
        for k in range(n):
            pc[it, q, k] = unwindow(pw, base + k, ext, start).astype(BF)

    def pair(it, q):
        return pltpu.make_async_remote_copy(
            src_ref=pc.at[it, q], dst_ref=sb.at[it],
            send_sem=sem_ps.at[it], recv_sem=sem_pr.at[it],
            device_id={"depth": sibling}, device_id_type=MESH,
        )

    def part(it, r):
        return pltpu.make_async_remote_copy(
            src_ref=qb.at[it, r], dst_ref=rb.at[it, r],
            send_sem=sem_rs.at[it, r], recv_sem=sem_rr.at[it, r],
            device_id={"depth": 2 * peers[r] + c}, device_id_type=MESH,
        )

    def shared_part(it, side, r):
        at = slice(2 * HALO, edge) if side == 0 else slice(0, 2 * HALO)
        return pltpu.make_async_remote_copy(
            src_ref=qb.at[it, r, at, :], dst_ref=ub.at[it, side, r],
            send_sem=sem_hs.at[it, side], recv_sem=sem_hr.at[it, side],
            device_id={"depth": 2 * peers[r] + c, "strip": (above, below)[side]},
            device_id_type=MESH,
        )

    def all_shared(it, side):
        return pltpu.make_async_remote_copy(
            src_ref=ub.at[it, side], dst_ref=ub.at[it, side],
            send_sem=sem_hs.at[it, side], recv_sem=sem_hr.at[it, side],
            device_id={"strip": (above, below)[side]}, device_id_type=MESH,
        )

    def slot(it, q, k):
        base, n = CHUNKS[it][q]
        if n == chips:
            return 1 + base + k
        return 1 + base + k + (k // n) * (nk + 1 - base - n)

    def give(it, at, target, send, recv):
        at = rc.at[it, at, 0:ext, :]
        return pltpu.make_async_remote_copy(
            src_ref=at, dst_ref=at, send_sem=send, recv_sem=recv,
            device_id={"depth": target}, device_id_type=MESH,
        )

    def to_chip(it, q, r):
        return give(it, slot(it, q, chip), 2 * peers[r] + c, sem_as.at[it, r], sem_ar.at[it, r])

    def from_chip(it, q, r):
        return give(it, slot(it, q, givers[r]), sibling, sem_as.at[it, r], sem_ar.at[it, r])

    def to_core(it, q, r):
        return give(it, slot(it, q, givers[r]), sibling, sem_fs.at[it, r], sem_fr.at[it, r])

    def pair_send(it, q):
        @pl.when(c != q)
        def _():
            pair(it, q).start()

    def part_send(it, q):
        @pl.when(c == q)
        def _():
            pair(it, q).wait_recv()
            for r in far + [0]:
                k = peers[r]
                qb[it, r] = (pc[it, q, k].astype(F32) + sb[it, k].astype(F32)).astype(BF)
                shared_part(it, 0, r).start()
                shared_part(it, 1, r).start()
                if r:
                    part(it, r).start()

    def ratio_send(it, q):
        @pl.when(c == q)
        def _():
            total = pc[it, q, chip].astype(F32) + sb[it, chip].astype(F32)
            for r in near:
                part(it, r).wait_recv()
                total = total + rb[it, r].astype(F32)
            m_up(it).wait_recv()
            m_down(it).wait_recv()
            all_shared(it, 0).wait_recv()
            all_shared(it, 1).wait_recv()
            shared = [ub[it, side, 0].astype(F32) for side in range(2)]
            for r in range(1, chips):
                shared = [shared[side] + ub[it, side, r].astype(F32) for side in range(2)]
            total = jnp.concatenate([
                total[0 : 2 * HALO] + jnp.where(s < strips - 1, shared[0], 0.0),
                total[2 * HALO : edge] + jnp.where(s > 0, shared[1], 0.0),
                total[edge:],
            ], axis=0)
            y = s * rows + strip_row(iota((ext, LANE), 0))
            ok = (y >= 0) & (y < rows * strips) & (chip < CHUNKS[it][q][1])
            mine = slot(it, q, chip)
            rc[it, mine, 0:ext, :] = jnp.where(ok, mc[it] / total, 0.0).astype(BF)
            for r in far:
                to_chip(it, q, r).start()
            to_core(it, q, 0).start()

    def ratio_forward(it, q):
        @pl.when(c == q)
        def _():
            for r in near:
                from_chip(it, q, r).wait_recv()
                to_core(it, q, r).start()

    def ratio_arrived(it, q):
        @pl.when(c != q)
        def _():
            for r in range(chips):
                to_core(it, q, r).wait_recv()

    def back(it, q):
        count = BACK[it][q]
        last = CHUNKS[it][q][0] + CHUNKS[it][q][1]
        for b in range(count):
            at, sh = divmod(LANE - RMAX + FIRST[q] + BW * b, LANE)
            pieces = [
                rc[it, at + i].astype(F32)
                if at + i <= last or q == 1 else jnp.zeros((kext, LANE), F32)
                for i in range(3)
            ]
            x = jnp.concatenate(pieces, axis=1)
            if sh:
                x = pltpu.roll(x, WIN + LANE - sh, axis=1)
            wr[kext * b : kext * (b + 1), :] = x[:, :WIN].astype(BF)
        lo = SPLIT[it] if q == 1 else 0
        hi = SPLIT[it] if q == 0 else cols

        for z in range(planes):
            for g, n in groups(count):
                res = dot(wr[kext * g : kext * (g + n), :], gm[z])
                for i in range(n):
                    ga[z % 2, :, WIN * (g + i) : WIN * (g + i + 1)] = (
                        res[kext * i : kext * (i + 1)].astype(BF)
                    )
            scale = jnp.concatenate([rinv[z], rinv[z]], axis=1)
            for b in range(count):
                bp = dot(bt[z], ga[z % 2, :, WIN * b : WIN * (b + 1)])
                row = MOST * q + b
                bpw[z % 2, :, WIN * b : WIN * (b + 1)] = bp * scale * cinv[z, row : row + 1, :]
            for k in range(lo // LANE, -(-hi // LANE)):
                at = slice(LANE * (k + 1), LANE * (k + 2))
                factor = unwindow(bpw.at[z % 2], k, LANE, FIRST[q])
                x = iota(factor.shape, 1) + LANE * k
                if LANE * k < lo:
                    factor = jnp.where(x >= lo, factor, 1.0)
                if LANE * (k + 1) > hi:
                    factor = jnp.where(x < hi, factor, 1.0)
                v32[z, :, at] = v32[z, :, at] * factor
            if it == ITERS - 1 and q == 1:
                vol_out(z).start()

    def forward(it, q):
        spread(it, q)
        if it == 0 and q == 1:
            part_send(it, 0)
        sensor_part(it, q)
        if it == 0 and q == 0:
            meet()
        pair_send(it, q)
        if it > 0 or q == 1:
            part_send(it, q)

    forward(0, 0)
    forward(0, 1)
    back_operators()
    for it in range(ITERS):
        ratio_send(it, 0)
        ratio_send(it, 1)
        ratio_forward(it, 0)
        ratio_arrived(it, 0)
        back(it, 0)
        if it + 1 < ITERS:
            forward(it + 1, 0)
        ratio_forward(it, 1)
        ratio_arrived(it, 1)
        back(it, 1)
        if it + 1 < ITERS:
            forward(it + 1, 1)

    for it in range(ITERS):
        m_up(it).wait_send()
        m_down(it).wait_send()
        for q in range(2):
            @pl.when(c != q)
            def _():
                pair(it, q).wait_send()

            @pl.when(c == q)
            def _():
                all_shared(it, 0).wait_send()
                all_shared(it, 1).wait_send()
                for r in range(1, chips):
                    part(it, r).wait_send()
                    to_chip(it, q, r).wait_send()
                for r in range(chips):
                    to_core(it, q, r).wait_send()
    for z in range(planes):
        vol_out(z).wait()


def local(depths, strips, volume, measured, row_taps, col_taps, phase_map, radius):
    planes, rows, cols = volume.shape
    ext = rows + 2 * HALO
    kext = 160
    nk = cols // LANE
    chips = depths // 2
    dma = pltpu.SemaphoreType.DMA
    vmem = pltpu.VMEM
    return pl.pallas_call(
        functools.partial(kernel, depths, strips),
        out_shape=jax.ShapeDtypeStruct(volume.shape, F32),
        in_specs=[pl.BlockSpec(memory_space=pltpu.HBM)] * 6,
        out_specs=pl.BlockSpec(memory_space=pl.ANY),
        scratch_shapes=[
            vmem(row_taps.shape, F32),
            vmem((PITCH, planes, TAPS), F32),
            pltpu.SMEM(phase_map.shape, jnp.int32),
            pltpu.SMEM(radius.shape, jnp.int32),
            vmem((planes, LANE, cols + 2 * LANE), F32),
            vmem((planes * LANE, MOST * WIN), BF),
            vmem((kext, MOST * WIN), F32),
            vmem((ITERS, 2, chips, ext, LANE), BF),
            vmem((ITERS, chips, ext, LANE), BF),
            vmem((ITERS, chips, ext, LANE), BF),
            vmem((ITERS, chips, ext, LANE), BF),
            vmem((ITERS, 2, chips, 2 * HALO, LANE), BF),
            vmem((ITERS, ext, LANE), F32),
            vmem((ITERS, nk + 3, kext, LANE), BF),
            vmem((MOST * kext, WIN), BF),
            vmem((2, kext, MOST * WIN), BF),
            vmem((2, LANE, MOST * WIN), F32),
            vmem((planes, LANE, LANE), F32),
            vmem((planes, LANE, LANE), F32),
            vmem((planes, WIN, LANE), F32),
            vmem((planes, WIN, WIN), BF),
            vmem((planes, WIN, WIN), BF),
            vmem((planes, LANE, kext), BF),
            vmem((kext, planes * LANE), BF),
            vmem((planes, 16, WIN), F32),
            vmem((planes, LANE, LANE), F32),
            dma((planes,)),
            dma((planes,)),
            dma((4 + 2 * ITERS,)),
            dma((ITERS, 2)),
            dma((ITERS, 2)),
            dma((ITERS,)),
            dma((ITERS,)),
            dma((ITERS, chips)),
            dma((ITERS, chips)),
            dma((ITERS, 2)),
            dma((ITERS, 2)),
            dma((ITERS, chips)),
            dma((ITERS, chips)),
            dma((ITERS, chips)),
            dma((ITERS, chips)),
        ],
        compiler_params=pltpu.CompilerParams(
            collective_id=0, has_side_effects=True, vmem_limit_bytes=48 * 1024 * 1024
        ),
    )(*(
        pltpu.with_memory_space_constraint(x, pltpu.HBM)
        for x in (volume, measured, row_taps, jnp.transpose(col_taps, (1, 0, 2)), phase_map, radius)
    ))


def solution(mesh):
    return jax.shard_map(
        functools.partial(local, mesh.shape["depth"], mesh.shape["strip"]),
        mesh=mesh,
        in_specs=(
            P("depth", "strip", None),
            P("strip", None),
            P("depth", None),
            P("depth", None, None),
            P("depth", None),
            P("depth"),
        ),
        out_specs=P("depth", "strip", None),
        check_vma=False,
    )
```

```python
import functools

import jax
import jax.numpy as jnp
from jax import lax
from jax.experimental import pallas as pl
from jax.experimental.pallas import tpu as pltpu
from jax.sharding import PartitionSpec as P

PITCH = 15
RMAX = 15
TAPS = 2 * RMAX + 1
ITERS = 2
LANE = 128
WIN = 256
BW = 225
FIRST = (0, 795)
SPREAD = (((0, 5), (1, 4)), ((0, 4), (0, 5)))
CHUNKS = (((0, 8), (8, 7)), ((0, 7), (7, 8)))
BACK = ((5, 5), (4, 5))
SPLIT = (1005, 870)
MOST = 5
HALO = 16
MESH = pl.DeviceIdType.MESH
BF = jnp.bfloat16
F32 = jnp.float32


def iota(shape, axis):
    return lax.broadcasted_iota(jnp.int32, shape, axis)


def dot(a, b):
    return jnp.dot(a, b, preferred_element_type=F32)


def unwindow(ref, k, rows, start):
    b0, l0 = divmod(LANE * k - start, BW)
    if b0 < 0:
        return pltpu.roll(ref[:rows, 0:LANE], start - LANE * k, axis=1)
    n0 = min(LANE, BW - l0)
    base = WIN * b0
    if l0 == 0:
        a = ref[:rows, base : base + LANE]
    elif l0 < LANE:
        a = pltpu.roll(ref[:rows, base : base + WIN], WIN - l0, axis=1)[:, :LANE]
    elif l0 == LANE:
        a = ref[:rows, base + LANE : base + WIN]
    else:
        a = pltpu.roll(ref[:rows, base + LANE : base + WIN], WIN - l0, axis=1)
    if n0 < LANE:
        b = pltpu.roll(ref[:rows, base + WIN : base + WIN + LANE], n0, axis=1)
        a = jnp.where(iota(a.shape, 1) < n0, a, b)
    return a


def kernel(depths, strips, vol_hbm, meas_hbm, rt_hbm, ct_hbm, pm_hbm, rad_hbm, out_ref,
           rt_ref, ct_ref, pm_ref, rad_ref,
           v32, spr, pw, pc, sb, qb, rb, ub, mc, rc, wr, ga, bpw,
           ctf, up, tap_ref, fm, gm, bt, bfm, cinv, rinv,
           sem_vol, sem_in, sem_ms, sem_mr, sem_ps, sem_pr, sem_rs, sem_rr,
           sem_hs, sem_hr, sem_as, sem_ar, sem_fs, sem_fr):
    planes, rows, cols = vol_hbm.shape
    ext = rows + 2 * HALO
    kext = ga.shape[1]
    edge = 4 * HALO
    nk = cols // LANE
    chips = depths // 2
    d = lax.axis_index("depth")
    s = lax.axis_index("strip")
    c = lax.rem(d, 2)
    chip = d // 2
    sibling = d + 1 - 2 * c
    above = lax.rem(s + strips - 1, strips)
    below = lax.rem(s + 1, strips)
    ys = chips // 2
    xc, yc = chip // ys, lax.rem(chip, ys)
    peers = [lax.rem(xc + r // ys, 2) * ys + lax.rem(yc + r, ys) for r in range(chips)]
    givers = [lax.rem(xc + r // ys, 2) * ys + lax.rem(yc + ys - r % ys, ys) for r in range(chips)]
    near = sorted(range(1, chips), key=lambda r: 2 * (r // ys) + min(r % ys, ys - r % ys))
    far = near[::-1]

    barrier = pltpu.get_barrier_semaphore()
    pl.semaphore_signal(barrier, inc=1, device_id={"depth": sibling}, device_id_type=MESH)
    for r in range(1, chips):
        pl.semaphore_signal(
            barrier, inc=1, device_id={"depth": 2 * peers[r] + c}, device_id_type=MESH
        )
    for t in (above, below):
        for r in range(chips):
            pl.semaphore_signal(
                barrier, inc=1, device_id={"depth": 2 * peers[r] + c, "strip": t},
                device_id_type=MESH,
            )

    def strip_row(p):
        return jnp.where(p < 2 * HALO, p + rows - HALO, p - 3 * HALO)

    arg_in = []
    for i, (src, dst) in enumerate(
        ((rt_hbm, rt_ref), (ct_hbm, ct_ref), (pm_hbm, pm_ref), (rad_hbm, rad_ref))
    ):
        copy = pltpu.make_async_copy(src, dst, sem_in.at[i])
        copy.start()
        arg_in.append(copy)
    def vol_in(z):
        return pltpu.make_async_copy(
            vol_hbm.at[z], v32.at[z, 0:rows, LANE : LANE + cols], sem_vol.at[z]
        )

    for z in range(planes):
        vol_in(z).start()
    mc_in = []
    for it in range(ITERS):
        mine = CHUNKS[it][0][0] + (CHUNKS[it][1][0] - CHUNKS[it][0][0]) * c + chip
        col0 = pl.multiple_of(jnp.minimum(mine, nk - 1) * LANE, LANE)
        mc_in.append(pltpu.make_async_copy(
            meas_hbm.at[0 : rows - HALO, pl.ds(col0, LANE)],
            mc.at[it, 3 * HALO : ext, :], sem_in.at[4 + 2 * it],
        ))
        mc_in.append(pltpu.make_async_copy(
            meas_hbm.at[rows - HALO : rows, pl.ds(col0, LANE)],
            mc.at[it, 0:HALO, :], sem_in.at[5 + 2 * it],
        ))
    for copy in mc_in:
        copy.start()

    for z in range(planes):
        v32[z, rows:, :] = jnp.zeros((LANE - rows, v32.shape[2]), F32)
        v32[z, :, 0:LANE] = jnp.zeros((LANE, LANE), F32)
        v32[z, :, LANE + cols :] = jnp.zeros((LANE, v32.shape[2] - LANE - cols), F32)
    for it in range(ITERS):
        for q in range(2):
            for k in range(CHUNKS[it][q][1], chips):
                pc[it, q, k] = jnp.zeros((ext, LANE), BF)
        rc[it, 0] = jnp.zeros((kext, LANE), BF)
        rc[it, nk + 1] = jnp.zeros((kext, LANE), BF)
        for k in range(1, nk + 1):
            rc[it, k, ext:, :] = jnp.zeros((kext - ext, LANE), BF)

    up[...] = jnp.zeros_like(up)
    ctf[...] = jnp.zeros_like(ctf)
    every = jnp.where(lax.rem(iota((WIN, LANE), 0), PITCH) == iota((WIN, LANE), 1), 1.0, 0.0)
    every = every.astype(BF)
    for copy in arg_in:
        copy.wait()
    for z in range(planes):
        reach = rad_ref[z]
        keep = jnp.abs(iota((PITCH, TAPS), 1) - RMAX) <= reach
        ctf[z, 0:PITCH, 0:TAPS] = jnp.where(keep, ct_ref[:, z, :], 0.0)
        keep1 = jnp.abs(iota((1, TAPS), 1) - RMAX) <= reach
        ctf[z, 16:17, 0:TAPS] = jnp.where(keep1, rt_ref[z : z + 1, :], 0.0)
        family = jnp.full((16, LANE), -1, jnp.int32)
        for p in range(PITCH):
            family = jnp.where(iota((16, LANE), 0) == p, pm_ref[z, p], family)
        pick = jnp.where(family == iota((16, LANE), 1), 1.0, 0.0).astype(BF)
        table = ctf[z].astype(BF)
        up[z, 0:16, :] = dot(pick, table)
        taps = dot(every, up[z].astype(BF))
        tap_ref[z] = taps
        taps = jnp.concatenate([taps, jnp.zeros((WIN, WIN - LANE), F32)], axis=1)
        fwd = pltpu.roll(taps, 32 - 2 * RMAX, axis=1)
        fwd = pltpu.roll(fwd, WIN - 32, axis=1, stride=1, stride_axis=0)
        fm[z] = fwd.astype(BF)
        rtap = jnp.concatenate([ctf[z, 16:17, :], jnp.zeros((1, WIN - LANE), F32)], axis=1)
        rtap = jnp.broadcast_to(rtap, (LANE, WIN))
        band = pltpu.roll(rtap, 1, axis=1)
        band = pltpu.roll(band, 0, axis=1, stride=1, stride_axis=0)
        p = iota((LANE, WIN), 1)
        last = pltpu.roll(band, WIN - rows, axis=1)
        band = jnp.where(p < 2 * HALO, last, pltpu.roll(band, 2 * HALO, axis=1))
        band = jnp.where(p < ext, band, 0.0)
        bt[z] = band[:, :kext].astype(BF)
        bfm[:, LANE * z : LANE * (z + 1)] = jnp.transpose(band)[:kext, :].astype(BF)

    def back_operators():
        y = s * rows + strip_row(iota((kext, LANE), 0))
        inside = (y >= 0) & (y < rows * strips) & (iota((kext, LANE), 0) < ext)
        inside = jnp.where(inside, 1.0, 0.0).astype(BF)
        block = iota((16, WIN), 0)
        xo = jnp.where(block < MOST, FIRST[0] + BW * block, FIRST[1] + BW * (block - MOST))
        xo = xo + iota((16, WIN), 1)
        xs = xo - RMAX
        ones_win = jnp.where((xs >= 0) & (xs < cols), 1.0, 0.0).astype(BF)
        col_ok = (xo < cols) & (iota((16, WIN), 1) < BW)
        row_ok = iota((LANE, LANE), 0) < rows
        for z in range(planes):
            taps = jnp.concatenate([tap_ref[z], jnp.zeros((WIN, WIN - LANE), F32)], axis=1)
            taps = pltpu.roll(taps, 0, axis=1, stride=1, stride_axis=0)
            gm[z] = jnp.transpose(taps).astype(BF)
            rn = dot(bt[z], inside)
            rinv[z] = jnp.where(row_ok, 1.0 / rn, 0.0)
            cn = dot(ones_win, gm[z])
            cinv[z] = jnp.where(col_ok, 1.0 / cn, 0.0)

    def m_up(it):
        return pltpu.make_async_remote_copy(
            src_ref=mc.at[it, 3 * HALO : 4 * HALO, :], dst_ref=mc.at[it, HALO : 2 * HALO, :],
            send_sem=sem_ms.at[it, 0], recv_sem=sem_mr.at[it, 0],
            device_id={"strip": above}, device_id_type=MESH,
        )

    def m_down(it):
        return pltpu.make_async_remote_copy(
            src_ref=mc.at[it, 0:HALO, :], dst_ref=mc.at[it, 2 * HALO : 3 * HALO, :],
            send_sem=sem_ms.at[it, 1], recv_sem=sem_mr.at[it, 1],
            device_id={"strip": below}, device_id_type=MESH,
        )

    def meet():
        pl.semaphore_wait(barrier, 3 * chips)
        for copy in mc_in:
            copy.wait()
        for it in range(ITERS):
            m_up(it).start()
            m_down(it).start()

    def groups(count):
        return [(g, min(3, count - g)) for g in range(0, count, 3)]

    def window(z, start):
        q, sh = divmod(LANE - RMAX + start, LANE)
        x = v32[z, :, LANE * q : LANE * q + WIN + LANE]
        if sh:
            x = pltpu.roll(x, WIN + LANE - sh, axis=1)
        return x[:, :WIN].astype(BF)

    def spread(it, q):
        first, count = SPREAD[it][q]
        start = FIRST[q] + BW * first

        for z in range(planes):
            if it == 0 and q == 0:
                vol_in(z).wait()
            for g, n in groups(count):
                lhs = jnp.concatenate([window(z, start + BW * (g + i)) for i in range(n)], axis=0)
                res = dot(lhs, fm[z])
                for i in range(n):
                    spr[z * LANE : (z + 1) * LANE,
                        WIN * (g + i) : WIN * (g + i + 1)] = (
                        res[LANE * i : LANE * (i + 1)].astype(BF)
                    )

    def sensor_part(it, q):
        first, count = SPREAD[it][q]
        start = FIRST[q] + BW * first
        for b in range(count):
            pw[:, WIN * b : WIN * (b + 1)] = dot(bfm[...], spr[:, WIN * b : WIN * (b + 1)])
        base, n = CHUNKS[it][q]
        for k in range(n):
            pc[it, q, k] = unwindow(pw, base + k, ext, start).astype(BF)

    def pair(it, q):
        return pltpu.make_async_remote_copy(
            src_ref=pc.at[it, q], dst_ref=sb.at[it],
            send_sem=sem_ps.at[it], recv_sem=sem_pr.at[it],
            device_id={"depth": sibling}, device_id_type=MESH,
        )

    def part(it, r):
        return pltpu.make_async_remote_copy(
            src_ref=qb.at[it, r], dst_ref=rb.at[it, r],
            send_sem=sem_rs.at[it, r], recv_sem=sem_rr.at[it, r],
            device_id={"depth": 2 * peers[r] + c}, device_id_type=MESH,
        )

    def shared_part(it, side, r):
        at = slice(2 * HALO, edge) if side == 0 else slice(0, 2 * HALO)
        return pltpu.make_async_remote_copy(
            src_ref=qb.at[it, r, at, :], dst_ref=ub.at[it, side, r],
            send_sem=sem_hs.at[it, side], recv_sem=sem_hr.at[it, side],
            device_id={"depth": 2 * peers[r] + c, "strip": (above, below)[side]},
            device_id_type=MESH,
        )

    def all_shared(it, side):
        return pltpu.make_async_remote_copy(
            src_ref=ub.at[it, side], dst_ref=ub.at[it, side],
            send_sem=sem_hs.at[it, side], recv_sem=sem_hr.at[it, side],
            device_id={"strip": (above, below)[side]}, device_id_type=MESH,
        )

    def slot(it, q, k):
        base, n = CHUNKS[it][q]
        if n == chips:
            return 1 + base + k
        return 1 + base + k + (k // n) * (nk + 1 - base - n)

    def give(it, at, target, send, recv):
        at = rc.at[it, at, 0:ext, :]
        return pltpu.make_async_remote_copy(
            src_ref=at, dst_ref=at, send_sem=send, recv_sem=recv,
            device_id={"depth": target}, device_id_type=MESH,
        )

    def to_chip(it, q, r):
        return give(it, slot(it, q, chip), 2 * peers[r] + c, sem_as.at[it, r], sem_ar.at[it, r])

    def from_chip(it, q, r):
        return give(it, slot(it, q, givers[r]), sibling, sem_as.at[it, r], sem_ar.at[it, r])

    def to_core(it, q, r):
        return give(it, slot(it, q, givers[r]), sibling, sem_fs.at[it, r], sem_fr.at[it, r])

    def pair_send(it, q):
        @pl.when(c != q)
        def _():
            pair(it, q).start()

    def part_send(it, q):
        @pl.when(c == q)
        def _():
            pair(it, q).wait_recv()
            for r in far + [0]:
                k = peers[r]
                qb[it, r] = (pc[it, q, k].astype(F32) + sb[it, k].astype(F32)).astype(BF)
                shared_part(it, 0, r).start()
                shared_part(it, 1, r).start()
                if r:
                    part(it, r).start()

    def ratio_send(it, q):
        @pl.when(c == q)
        def _():
            total = pc[it, q, chip].astype(F32) + sb[it, chip].astype(F32)
            for r in near:
                part(it, r).wait_recv()
                total = total + rb[it, r].astype(F32)
            m_up(it).wait_recv()
            m_down(it).wait_recv()
            all_shared(it, 0).wait_recv()
            all_shared(it, 1).wait_recv()
            shared = [ub[it, side, 0].astype(F32) for side in range(2)]
            for r in range(1, chips):
                shared = [shared[side] + ub[it, side, r].astype(F32) for side in range(2)]
            total = jnp.concatenate([
                total[0 : 2 * HALO] + jnp.where(s < strips - 1, shared[0], 0.0),
                total[2 * HALO : edge] + jnp.where(s > 0, shared[1], 0.0),
                total[edge:],
            ], axis=0)
            y = s * rows + strip_row(iota((ext, LANE), 0))
            ok = (y >= 0) & (y < rows * strips) & (chip < CHUNKS[it][q][1])
            mine = slot(it, q, chip)
            rc[it, mine, 0:ext, :] = jnp.where(ok, mc[it] / total, 0.0).astype(BF)
            for r in far:
                to_chip(it, q, r).start()
            to_core(it, q, 0).start()

    def ratio_forward(it, q):
        @pl.when(c == q)
        def _():
            for r in near:
                from_chip(it, q, r).wait_recv()
                to_core(it, q, r).start()

    def ratio_arrived(it, q):
        @pl.when(c != q)
        def _():
            for r in range(chips):
                to_core(it, q, r).wait_recv()

    def back(it, q):
        count = BACK[it][q]
        last = CHUNKS[it][q][0] + CHUNKS[it][q][1]
        for b in range(count):
            at, sh = divmod(LANE - RMAX + FIRST[q] + BW * b, LANE)
            pieces = [
                rc[it, at + i].astype(F32)
                if at + i <= last or q == 1 else jnp.zeros((kext, LANE), F32)
                for i in range(3)
            ]
            x = jnp.concatenate(pieces, axis=1)
            if sh:
                x = pltpu.roll(x, WIN + LANE - sh, axis=1)
            wr[kext * b : kext * (b + 1), :] = x[:, :WIN].astype(BF)
        lo = SPLIT[it] if q == 1 else 0
        hi = SPLIT[it] if q == 0 else cols

        for z in range(planes):
            for g, n in groups(count):
                res = dot(wr[kext * g : kext * (g + n), :], gm[z])
                for i in range(n):
                    ga[z % 2, :, WIN * (g + i) : WIN * (g + i + 1)] = (
                        res[kext * i : kext * (i + 1)].astype(BF)
                    )
            scale = jnp.concatenate([rinv[z], rinv[z]], axis=1)
            for b in range(count):
                bp = dot(bt[z], ga[z % 2, :, WIN * b : WIN * (b + 1)])
                row = MOST * q + b
                bpw[z % 2, :, WIN * b : WIN * (b + 1)] = bp * scale * cinv[z, row : row + 1, :]
            for k in range(lo // LANE, -(-hi // LANE)):
                at = slice(LANE * (k + 1), LANE * (k + 2))
                factor = unwindow(bpw.at[z % 2], k, LANE, FIRST[q])
                x = iota(factor.shape, 1) + LANE * k
                if LANE * k < lo:
                    factor = jnp.where(x >= lo, factor, 1.0)
                if LANE * (k + 1) > hi:
                    factor = jnp.where(x < hi, factor, 1.0)
                new = v32[z, :, at] * factor
                if it == ITERS - 1 and LANE * (k + 1) <= hi:
                    out_ref[z, :, LANE * k : LANE * (k + 1)] = new[:rows]
                else:
                    v32[z, :, at] = new

    def forward(it, q):
        spread(it, q)
        if it == 0 and q == 1:
            part_send(it, 0)
        sensor_part(it, q)
        if it == 0 and q == 0:
            meet()
        pair_send(it, q)
        if it > 0 or q == 1:
            part_send(it, q)

    forward(0, 0)
    forward(0, 1)
    back_operators()
    for it in range(ITERS):
        ratio_send(it, 0)
        ratio_send(it, 1)
        ratio_forward(it, 0)
        ratio_arrived(it, 0)
        back(it, 0)
        if it + 1 < ITERS:
            forward(it + 1, 0)
        ratio_forward(it, 1)
        ratio_arrived(it, 1)
        back(it, 1)
        if it + 1 < ITERS:
            forward(it + 1, 1)

    for it in range(ITERS):
        m_up(it).wait_send()
        m_down(it).wait_send()
        for q in range(2):
            @pl.when(c != q)
            def _():
                pair(it, q).wait_send()

            @pl.when(c == q)
            def _():
                all_shared(it, 0).wait_send()
                all_shared(it, 1).wait_send()
                for r in range(1, chips):
                    part(it, r).wait_send()
                    to_chip(it, q, r).wait_send()
                for r in range(chips):
                    to_core(it, q, r).wait_send()


def local(depths, strips, volume, measured, row_taps, col_taps, phase_map, radius):
    planes, rows, cols = volume.shape
    ext = rows + 2 * HALO
    kext = 160
    nk = cols // LANE
    chips = depths // 2
    dma = pltpu.SemaphoreType.DMA
    vmem = pltpu.VMEM
    return pl.pallas_call(
        functools.partial(kernel, depths, strips),
        out_shape=jax.ShapeDtypeStruct(volume.shape, F32),
        in_specs=[pl.BlockSpec(memory_space=pltpu.HBM)] * 6,
        out_specs=pl.BlockSpec(memory_space=pltpu.VMEM),
        scratch_shapes=[
            vmem(row_taps.shape, F32),
            vmem((PITCH, planes, TAPS), F32),
            pltpu.SMEM(phase_map.shape, jnp.int32),
            pltpu.SMEM(radius.shape, jnp.int32),
            vmem((planes, LANE, cols + 2 * LANE), F32),
            vmem((planes * LANE, MOST * WIN), BF),
            vmem((kext, MOST * WIN), F32),
            vmem((ITERS, 2, chips, ext, LANE), BF),
            vmem((ITERS, chips, ext, LANE), BF),
            vmem((ITERS, chips, ext, LANE), BF),
            vmem((ITERS, chips, ext, LANE), BF),
            vmem((ITERS, 2, chips, 2 * HALO, LANE), BF),
            vmem((ITERS, ext, LANE), F32),
            vmem((ITERS, nk + 3, kext, LANE), BF),
            vmem((MOST * kext, WIN), BF),
            vmem((2, kext, MOST * WIN), BF),
            vmem((2, LANE, MOST * WIN), F32),
            vmem((planes, LANE, LANE), F32),
            vmem((planes, LANE, LANE), F32),
            vmem((planes, WIN, LANE), F32),
            vmem((planes, WIN, WIN), BF),
            vmem((planes, WIN, WIN), BF),
            vmem((planes, LANE, kext), BF),
            vmem((kext, planes * LANE), BF),
            vmem((planes, 16, WIN), F32),
            vmem((planes, LANE, LANE), F32),
            dma((planes,)),
            dma((4 + 2 * ITERS,)),
            dma((ITERS, 2)),
            dma((ITERS, 2)),
            dma((ITERS,)),
            dma((ITERS,)),
            dma((ITERS, chips)),
            dma((ITERS, chips)),
            dma((ITERS, 2)),
            dma((ITERS, 2)),
            dma((ITERS, chips)),
            dma((ITERS, chips)),
            dma((ITERS, chips)),
            dma((ITERS, chips)),
        ],
        compiler_params=pltpu.CompilerParams(
            collective_id=0, has_side_effects=True, vmem_limit_bytes=48 * 1024 * 1024
        ),
    )(*(
        pltpu.with_memory_space_constraint(x, pltpu.HBM)
        for x in (volume, measured, row_taps, jnp.transpose(col_taps, (1, 0, 2)), phase_map, radius)
    ))


def solution(mesh):
    return jax.shard_map(
        functools.partial(local, mesh.shape["depth"], mesh.shape["strip"]),
        mesh=mesh,
        in_specs=(
            P("depth", "strip", None),
            P("strip", None),
            P("depth", None),
            P("depth", None, None),
            P("depth", None),
            P("depth"),
        ),
        out_specs=P("depth", "strip", None),
        check_vma=False,
    )
```
